512 devices in a mesh: dp: 2 (over z_hi), row: 16 (over y, core), col: 16 (over x, z_lo).
Axes of the slice: x: 4, y: 8, z: 8 (z_hi: 2, z_lo: 4; z = z_hi * 4 + z_lo), core: 2. Of those that a mesh axis runs over, the one named last changes fastest.
Arguments:
- tokens: bfloat16 [512, 8192], P(('dp', 'col'), 'row'), may hold values from -6 to 6
- cotangent: bfloat16 [512, 8192], P(('dp', 'col'), 'row'), may hold values from -6 to 6
- gate_blocks: bfloat16 [16, 16, 21, 128, 128], P('row', 'col'), may hold values from -0.09375 to 0.09375
- gate_index: int32 [16, 16, 21, 2], P('row', 'col'), may hold values from -1 to 6, as said below
- up_blocks: bfloat16 [16, 16, 21, 128, 128], P('row', 'col'), may hold values from -0.09375 to 0.09375
- up_index: int32 [16, 16, 21, 2], P('row', 'col'), may hold values from -1 to 6, as said below
- down_blocks: bfloat16 [16, 16, 21, 128, 128], P('row', 'col'), may hold values from -0.0625 to 0.0625
- down_index: int32 [16, 16, 21, 2], P('row', 'col'), may hold values from -1 to 6, as said below
Outputs:
- output: bfloat16 [512, 8192], P(('dp', 'col'), 'row')
- input_grad: bfloat16 [512, 8192], P(('dp', 'col'), 'row')
- gate_grad: bfloat16 [16, 16, 21, 128, 128], P('row', 'col')
- up_grad: bfloat16 [16, 16, 21, 128, 128], P('row', 'col')
- down_grad: bfloat16 [16, 16, 21, 128, 128], P('row', 'col')
The draws below stay inside these ranges and needn't reach their ends.
Inputs may be any that keep to these rules, and one draw needn't show every extreme that they name: `gate_index`: in each tile the listed slots come first and name distinct positions, with a first entry below 4 and a second below 7; every slot after them holds -1 in both entries. A tile lists 7 to 21 blocks, and some tile lists exactly 21. `up_index`: as for gate_index, with a pattern of its own. `down_index`: as for gate_index with the entries' roles swapped: the first is below 7, the second below 4. A tile lists 7 to 21 blocks, and some tile lists exactly 21.
All inputs are finite; a program needn't handle non-finite values.
Results may differ from the reference program's by a relative error of at most 0.0059.
Values may be sent and summed in bfloat16 or wider, within the bound.
A program may use at most 64 MiB of HBM per device.

```python
import jax
import jax.numpy as jnp
from jax import lax

D = 8192
FF = 14336
BLK = 128
TOK = 256
TOKENS = 512
DB = 4
FB = 7
SLOTS = 28
CAP = 21
LOW = 7
N_DP = 2
N_ROW = 16
N_COL = 16


def block_list(key, second_per):
    tiles = N_ROW * N_COL
    tile_keys = jax.random.split(key, tiles)
    orders = jax.vmap(lambda each_key: jax.random.permutation(each_key, SLOTS))(tile_keys)[:, :CAP]
    counts = jax.random.randint(jax.random.fold_in(key, 7), (tiles,), LOW, CAP + 1)
    fullest = jax.random.randint(jax.random.fold_in(key, 11), (), 0, tiles)
    counts = jnp.where(jnp.arange(tiles) == fullest, CAP, counts)
    used = jnp.arange(CAP)[None, :] < counts[:, None]
    first = jnp.where(used, orders // second_per, -1)
    second = jnp.where(used, orders % second_per, -1)
    return jnp.stack([first, second], axis=-1).astype(jnp.int32).reshape(N_ROW, N_COL, CAP, 2)


def draw_gate_index(key, part):
    return block_list(jax.random.fold_in(key, 1), FB)


def draw_up_index(key, part):
    return block_list(jax.random.fold_in(key, 2), FB)


def draw_down_index(key, part):
    return block_list(jax.random.fold_in(key, 3), DB)


def shard_levels(own_key, dims, cuts, low, high):
    def one(position, blocks):
        steps = jax.random.uniform(jax.random.fold_in(jax.random.fold_in(own_key, 6), position), (blocks,), jnp.float32, low / len(cuts), high / len(cuts))
        return jnp.repeat(jnp.exp(steps), dims[position] // blocks).reshape((-1,) + (1,) * (len(dims) - position - 1))

    gain = one(*cuts[0])
    for cut in cuts[1:]:
        gain = gain * one(*cut)
    return gain


def noise(rng, dims, deviation, reach, shards=(), kind=jnp.bfloat16):
    loudness = shard_levels(rng, dims, shards, -0.22, 0.18) if shards else 1.0
    result = jax.random.normal(rng, dims, jnp.float32) * deviation * loudness
    return jnp.minimum(jnp.maximum(result, -reach), reach).astype(kind)


def setup_inputs(seed: int = 0) -> dict:
    arg_keys = jax.random.split(jax.random.key(seed), 9)
    return {
        "tokens": noise(arg_keys[0], (TOKENS, D), 1.0, 6.0, ((0, 32), (1, 16))),
        "cotangent": noise(arg_keys[1], (TOKENS, D), 1.0, 6.0, ((0, 32), (1, 16))),
        "gate_blocks": noise(arg_keys[2], (N_ROW, N_COL, CAP, BLK, BLK), (D // 2) ** -0.5, 0.09375, ((0, 16), (1, 16))),
        "gate_index": draw_gate_index(jax.random.fold_in(arg_keys[8], 71), 0),
        "up_blocks": noise(arg_keys[4], (N_ROW, N_COL, CAP, BLK, BLK), (D // 2) ** -0.5, 0.09375, ((0, 16), (1, 16))),
        "up_index": draw_up_index(jax.random.fold_in(arg_keys[8], 71), 0),
        "down_blocks": noise(arg_keys[6], (N_ROW, N_COL, CAP, BLK, BLK), (FF // 2) ** -0.5, 0.0625, ((0, 16), (1, 16))),
        "down_index": draw_down_index(jax.random.fold_in(arg_keys[8], 71), 0),
    }


def tile_positions(index_list, first_per, second_per):
    used = index_list[..., 0] >= 0
    first_at = jnp.arange(index_list.shape[0], dtype=jnp.int32)[:, None, None] * first_per + jnp.maximum(index_list[..., 0], 0).astype(jnp.int32)
    second_at = jnp.arange(index_list.shape[1], dtype=jnp.int32)[None, :, None] * second_per + jnp.maximum(index_list[..., 1], 0).astype(jnp.int32)
    return used, first_at, second_at


def densify(blocks, index_list, first_per, second_per):
    used, first_at, second_at = tile_positions(index_list, first_per, second_per)
    first_total = index_list.shape[0] * first_per
    second_total = index_list.shape[1] * second_per
    values = jnp.where(used[..., None, None], blocks.astype(jnp.float32), jnp.float32(0.0))
    grid = jnp.zeros((first_total, second_total, BLK, BLK), jnp.float32)
    grid = grid.at[first_at, second_at].add(values)
    return grid.transpose(0, 2, 1, 3).reshape(first_total * BLK, second_total * BLK).astype(jnp.bfloat16)


def extract(full, index_list, first_per, second_per):
    used, first_at, second_at = tile_positions(index_list, first_per, second_per)
    shaped = full.reshape(index_list.shape[0] * first_per, BLK, index_list.shape[1] * second_per, BLK)
    picked = shaped[first_at, :, second_at, :]
    return jnp.where(used[..., None, None], picked, jnp.float32(0.0))


def contract_last(left, right):
    return lax.dot_general(left, right, (((1,), (1,)), ((), ())), preferred_element_type=jnp.float32)


def contract_first(left, right):
    return lax.dot_general(left, right, (((0,), (0,)), ((), ())), preferred_element_type=jnp.float32)


def reference(tokens, cotangent, gate_blocks, gate_index, up_blocks, up_index, down_blocks, down_index):
    w_gate = densify(gate_blocks, gate_index, DB, FB)
    w_up = densify(up_blocks, up_index, DB, FB)
    down_swapped = down_index.transpose(1, 0, 2, 3)
    w_down = densify(down_blocks.transpose(1, 0, 2, 3, 4), down_swapped, FB, DB)
    scale = 1.0 / (TOKENS ** 0.5)
    outputs = []
    input_grads = []
    gate_total = jnp.zeros(gate_blocks.shape, jnp.float32)
    up_total = jnp.zeros(up_blocks.shape, jnp.float32)
    down_total = jnp.zeros(down_blocks.shape, jnp.float32)
    for group in range(N_DP):
        inputs = tokens[group * TOK:(group + 1) * TOK]
        cotan = cotangent[group * TOK:(group + 1) * TOK]
        gate = jnp.dot(inputs, w_gate, preferred_element_type=jnp.float32)
        up = jnp.dot(inputs, w_up, preferred_element_type=jnp.float32)
        sigma = jax.nn.sigmoid(gate)
        hidden = (gate * sigma * up).astype(jnp.bfloat16)
        outputs.append(jnp.dot(hidden, w_down, preferred_element_type=jnp.float32).astype(jnp.bfloat16))
        grad_hidden = contract_last(cotan, w_down)
        grad_gate = (grad_hidden * up * sigma * (1.0 + gate * (1.0 - sigma))).astype(jnp.bfloat16)
        grad_up = (grad_hidden * gate * sigma).astype(jnp.bfloat16)
        summed = contract_last(grad_gate, w_gate) + contract_last(grad_up, w_up)
        input_grads.append(summed.astype(jnp.bfloat16))
        part_gate = (extract(contract_first(inputs, grad_gate), gate_index, DB, FB) * scale).astype(jnp.bfloat16)
        part_up = (extract(contract_first(inputs, grad_up), up_index, DB, FB) * scale).astype(jnp.bfloat16)
        part_down = (extract(contract_first(hidden, cotan), down_swapped, FB, DB).transpose(1, 0, 2, 3, 4) * scale).astype(jnp.bfloat16)
        part_gate, part_up, part_down = lax.optimization_barrier((part_gate, part_up, part_down))
        gate_total = gate_total + part_gate.astype(jnp.float32)
        up_total = up_total + part_up.astype(jnp.float32)
        down_total = down_total + part_down.astype(jnp.float32)
    return (jnp.concatenate(outputs, axis=0), jnp.concatenate(input_grads, axis=0),
            gate_total.astype(jnp.bfloat16), up_total.astype(jnp.bfloat16), down_total.astype(jnp.bfloat16))
```

```python
import functools
import math

import jax
import jax.numpy as jnp
from jax import lax
from jax.experimental import pallas as pl
from jax.experimental.pallas import tpu as pltpu
from jax.sharding import PartitionSpec as P

BLK = 128
XS = 4
MESH = pl.DeviceIdType.MESH
BF = jnp.bfloat16
F32 = jnp.float32


def split_tiles(tiles, parts, whole=False):
    cuts = [(tiles * i) // parts for i in range(parts + 1)]
    if whole:
        cuts = sorted({t * (tiles // 3) + c for t in range(3) for c in (0, (tiles // 3 + 1) // 2)} | {tiles})
        parts = len(cuts) - 1
    return [(cuts[i] * BLK, cuts[i + 1] * BLK, -1 if i % 2 == 0 else 1) for i in range(parts)]


class Dims:
    def __init__(self, mesh_shape, tok_rows, feat, cap, units):
        self.T = tok_rows
        self.F = feat
        self.CAP = cap
        self.DB = feat // BLK
        self.FB = units
        self.HU = units * BLK
        self.N = 3 * self.HU
        self.X = XS
        self.Z = mesh_shape["col"] // XS
        self.Y = mesh_shape["row"] // 2
        self.LONG = self.Y // 2
        self.SHORT = self.Y // 2 - 1
        self.NCOL = mesh_shape["col"]
        self.NROW = mesh_shape["row"]
        self.R = self.NCOL * self.T
        self.HALF = self.Y * self.T
        self.SL = self.DB * self.FB
        self.RS = split_tiles(3 * self.FB, 6, True)
        self.AG = split_tiles(3 * self.FB, 4)
        self.NSEM = 256


def main_kernel(
    d, gi, ui, di, tok, cot, gb, ub, db,
    o_out, ig_out, g_out, u_out, d_out,
    inv, wb0, wb1, wb2, wgu, wd, xr, xp, psend, precv, s1, rlong, slong, rshort, sshort, tot, hall,
    po, xsend, xrecv, zs, zsend, zrecv, fin, xt, ht, acc_gu, acc_d, dg, du, dd, pg, pu, pd,
    lsem, ssem, rsem,
):
    g = lax.axis_index("dp")
    row = lax.axis_index("row")
    col = lax.axis_index("col")
    y, k = lax.div(row, 2), lax.rem(row, 2)
    x, z = lax.div(col, d.Z), lax.rem(col, d.Z)
    T, F, HU, N, R = d.T, d.F, d.HU, d.N, d.R
    GU = 2 * HU
    ZT = d.Z * T
    wblk = (wb0, wb1, wb2)

    def ym(v):
        return lax.rem(y + v + 2 * d.Y, d.Y)

    def xm(v):
        return lax.rem(x + v + 2 * d.X, d.X)

    def zm(v):
        return lax.rem(z + v + 2 * d.Z, d.Z)

    def rows(start, size):
        return pl.ds(pl.multiple_of(start, size), size)

    def at_y(v):
        return {"row": ym(v) * 2 + k}

    def at_x(v):
        return {"col": xm(v) * d.Z + z}

    def at_z(v):
        return {"col": x * d.Z + zm(v)}

    def at_other_z(v):
        return {"dp": 1 - g, "col": x * d.Z + zm(v)}

    partner = {"row": y * 2 + 1 - k}

    sent = []
    ids = {}

    def number(name):
        if name not in ids:
            ids[name] = len(ids)
            assert len(ids) <= d.NSEM
        return ids[name]

    def send(name, src, dst, dev):
        i = number(name)
        c = pltpu.make_async_remote_copy(
            src_ref=src, dst_ref=dst, send_sem=ssem.at[i], recv_sem=rsem.at[i],
            device_id=dev, device_id_type=MESH,
        )
        c.start()
        sent.append(c)

    def recv(name, landing, dev):
        i = number(name)
        pltpu.make_async_remote_copy(
            src_ref=landing, dst_ref=landing, send_sem=ssem.at[i], recv_sem=rsem.at[i],
            device_id=dev, device_id_type=MESH,
        ).wait_recv()

    barrier = pltpu.get_barrier_semaphore()
    peers = [at_z(o) for o in range(1, d.Z)] + [at_other_z(o) for o in range(d.Z)]
    peers += [at_x(1), at_x(-1), at_y(1), at_y(-1), partner]
    for p in peers:
        pl.semaphore_signal(barrier, inc=1, device_id=p, device_id_type=MESH)

    own_rows = rows(col * T, T)
    loads = [
        pltpu.make_async_copy(tok, xr.at[0, own_rows], lsem.at[0]),
        pltpu.make_async_copy(cot, xr.at[1, own_rows], lsem.at[1]),
        pltpu.make_async_copy(gb, wb0.at[pl.ds(0, d.CAP)], lsem.at[2]),
        pltpu.make_async_copy(ub, wb1.at[pl.ds(0, d.CAP)], lsem.at[3]),
        pltpu.make_async_copy(db, wb2.at[pl.ds(0, d.CAP)], lsem.at[4]),
    ]
    for c in loads:
        c.start()

    pl.semaphore_wait(barrier, len(peers))

    def chunk(t, v, o):
        return xr.at[t, rows((xm(v) * d.Z + zm(-o)) * T, T)]

    def x_chunk(t, o, src):
        send(("xr", t, o), src, chunk(t, 0, o), at_x(1))
        send(("xl", t, o), src, chunk(t, 0, o), at_x(-1))

    def x_pass(t, o):
        m = 1 if t == 0 else -1
        side = "xr" if t == 0 else "xl"
        recv((side, t, o), chunk(t, -m, o), at_x(m))
        send(("xx", t, o), chunk(t, -m, o), chunk(t, -m, o), at_x(m))

    def x_end(t, o):
        m = 1 if t == 0 else -1
        side = "xl" if t == 0 else "xr"
        recv((side, t, o), chunk(t, m, o), at_x(-m))
        recv(("xx", t, o), chunk(t, 2, o), at_x(m))

    for t, src in ((0, tok), (1, cot)):
        for o in range(1, d.Z):
            send(("z0", t, o), src, xr.at[t, own_rows], at_z(o))
        x_chunk(t, 0, src)

    for t, (ref, per) in enumerate(((gi, d.FB), (ui, d.FB), (di, d.DB))):
        wblk[t][d.CAP] = jnp.zeros((BLK, BLK), BF)
        spots = [ref[0, s] * per + ref[1, s] for s in range(d.CAP)]

        def find(p, _, t=t, spots=spots):
            found = jnp.int32(d.CAP)
            for s in range(d.CAP):
                found = jnp.where(spots[s] == p, jnp.int32(s), found)
            inv[t * d.SL + p] = found
            return 0

        lax.fori_loop(0, d.SL, find, 0)

    def z_chunks(t):
        for o in range(1, d.Z):
            recv(("z0", t, o), chunk(t, 0, o), at_z(o))
            x_chunk(t, o, chunk(t, 0, o))

    def dense(t, per):
        loads[2 + t].wait()

        def put(p, _):
            i, j = lax.div(p, per), lax.rem(p, per)
            block = wblk[t][inv[t * d.SL + p]]
            if t < 2:
                wgu[rows(i * BLK, BLK), rows(j * BLK + t * HU, BLK)] = block
            else:
                wd[rows(i * BLK, BLK), rows(j * BLK, BLK)] = block
            return 0

        lax.fori_loop(0, d.SL, put, 0)

    z_chunks(0)
    z_chunks(1)

    other_rows = rows(R + col * T, T)
    for t, src in ((0, tok), (1, cot)):
        for o in range(d.Z):
            send(("z1", t, o), src, xr.at[t, other_rows], at_other_z(o))

    def z_other(t):
        for o in range(d.Z):
            recv(("z1", t, o), xr.at[t, rows(R + (x * d.Z + zm(-o)) * T, T)], at_z(o))

    def xblock(t, v):
        return xr.at[t, rows(R + xm(v) * ZT, ZT)]

    def b_send(t):
        send(("br", t), xblock(t, 0), xblock(t, 0), at_x(1))
        send(("bl", t), xblock(t, 0), xblock(t, 0), at_x(-1))

    def b_pass(t):
        m = 1 if t == 0 else -1
        recv(("br" if t == 0 else "bl", t), xblock(t, -m), at_x(m))
        send(("bb", t), xblock(t, -m), xblock(t, -m), at_x(m))

    def b_end(t):
        m = 1 if t == 0 else -1
        recv(("bl" if t == 0 else "br", t), xblock(t, m), at_x(-m))
        recv(("bb", t), xblock(t, 2), at_x(m))

    dense(0, d.FB)
    for o in range(d.Z):
        x_pass(0, o)
    dense(1, d.FB)
    for o in range(d.Z):
        x_pass(1, o)
    dense(2, d.DB)
    loads[0].wait()
    loads[1].wait()
    for t in (0, 1):
        for o in range(d.Z):
            x_end(t, o)

    def nt(a, b):
        return lax.dot_general(a, b, (((1,), (1,)), ((), ())), preferred_element_type=F32)

    def nn(a, b):
        return jnp.dot(a, b, preferred_element_type=F32)

    H = d.HALF
    for t in (0, 1):
        xp[t, 0:H] = xr[t, rows((1 - k) * H, H), :]
        xp[t, H : 2 * H] = xr[t, rows(k * H, H), :]
    for q, (a, b, _) in enumerate(d.RS):
        part = nn(xp[0], wgu[:, a:b]) if b <= GU else nt(xp[1], wd[a - GU : b - GU, :])
        psend[:, a:b] = part[0:H]
        send(("p", q), psend.at[:, a:b], precv.at[:, a:b], partner)
        s1[:, a:b] = part[H : 2 * H]

    def rs_long(s, q):
        a, b, m = d.RS[q]
        mine = s1[rows(ym(m * (d.LONG - s)) * T, T), a:b]
        if s > 0:
            recv(("rl", s - 1, q), rlong.at[s - 1, :, a:b], at_y(m))
            mine = mine + rlong[s - 1, :, a:b].astype(F32)
        slong[s, :, a:b] = mine.astype(BF)
        send(("rl", s, q), slong.at[s, :, a:b], rlong.at[s, :, a:b], at_y(m))

    def rs_short(s, q):
        a, b, m = d.RS[q]
        mine = s1[rows(ym(-m * (d.SHORT - s)) * T, T), a:b]
        if s > 0:
            recv(("rs", s - 1, q), rshort.at[s - 1, :, a:b], at_y(-m))
            mine = mine + rshort[s - 1, :, a:b].astype(F32)
        sshort[s, :, a:b] = mine.astype(BF)
        send(("rs", s, q), sshort.at[s, :, a:b], rshort.at[s, :, a:b], at_y(-m))

    for s in range(d.LONG):
        for q, (a, b, _) in enumerate(d.RS):
            if s == 0:
                recv(("p", q), precv.at[:, a:b], partner)
                s1[:, a:b] += precv[:, a:b]
            rs_long(s, q)
            if s < d.SHORT:
                rs_short(s, q)
        if s == 0:
            for t in (0, 1):
                z_other(t)
                b_send(t)
            xt[:, 0:R] = xr[0, 0:R, :].T
        if s == d.LONG - 1:
            b_pass(0)
            b_pass(1)
    for q, (a, b, m) in enumerate(d.RS):
        mine = s1[rows(y * T, T), a:b]
        if d.SHORT > 0:
            recv(("rs", d.SHORT - 1, q), rshort.at[d.SHORT - 1, :, a:b], at_y(-m))
            mine = mine + rshort[d.SHORT - 1, :, a:b].astype(F32)
        recv(("rl", d.LONG - 1, q), rlong.at[d.LONG - 1, :, a:b], at_y(m))
        tot[:, a:b] = mine + rlong[d.LONG - 1, :, a:b].astype(F32)

    gate, up, gh = tot[:, 0:HU], tot[:, HU:GU], tot[:, GU:N]
    sig = jax.nn.sigmoid(gate)
    mine_rows = rows((k * d.Y + y) * T, T)
    hall[mine_rows, 0:HU] = (gate * sig * up).astype(BF)
    hall[mine_rows, HU:GU] = (gh * up * sig * (1.0 + gate * (1.0 - sig))).astype(BF)
    hall[mine_rows, GU:N] = (gh * gate * sig).astype(BF)

    def hrows(gs, kk, yy):
        return rows(gs * R + (kk * d.Y + yy) * T, T)

    def ag_send(gs, s, q, long):
        a, b, m = d.AG[q]
        m = m if long else -m
        ref = hall.at[hrows(gs, k, ym(-m * s)), a:b]
        send(("al" if long else "as", gs, s, q), ref, ref, at_y(m))

    def ag_recv(gs, s, q, long):
        a, b, m = d.AG[q]
        m = m if long else -m
        ref = hall.at[hrows(gs, k, ym(-m * s)), a:b]
        recv(("al" if long else "as", gs, s - 1, q), ref, at_y(m))

    def to_partner(gs, v):
        ref = hall.at[hrows(gs, k, ym(v))]
        send(("ap", gs, v), ref, ref, partner)

    def ag_start(gs):
        for q in range(len(d.AG)):
            ag_send(gs, 0, q, True)
            if d.SHORT > 0:
                ag_send(gs, 0, q, False)
        to_partner(gs, 0)

    def ag_step(gs, s):
        for q in range(len(d.AG)):
            ag_recv(gs, s, q, True)
            if s < d.LONG:
                ag_send(gs, s, q, True)
            if s <= d.SHORT:
                ag_recv(gs, s, q, False)
                if s < d.SHORT:
                    ag_send(gs, s, q, False)
        to_partner(gs, s)
        if s <= d.SHORT:
            to_partner(gs, -s)

    def ag_partner(gs):
        for v in range(-d.SHORT, d.LONG + 1):
            recv(("ap", gs, v), hall.at[hrows(gs, 1 - k, ym(v))], partner)

    ag_start(0)
    send("dp", hall.at[mine_rows], hall.at[hrows(1, k, y)], {"dp": 1 - g})
    for s in range(1, d.LONG):
        ag_step(0, s)
    recv("dp", hall.at[hrows(1, k, y)], {"dp": 1 - g})
    ag_start(1)
    ag_step(0, d.LONG)
    ag_partner(0)

    def xrows(v):
        return rows(xm(v) * ZT, ZT)

    def x_first(t, m):
        a, b = t * F, (t + 1) * F
        xsend[t, 0] = po[xrows(2), a:b].astype(BF)
        send(("o0", t), xsend.at[t, 0], xrecv.at[t, 0], at_x(m))
        xsend[t, 1] = po[xrows(-m), a:b].astype(BF)
        send(("o1", t), xsend.at[t, 1], xrecv.at[t, 1], at_x(-m))

    def x_second(t, m):
        a, b = t * F, (t + 1) * F
        recv(("o0", t), xrecv.at[t, 0], at_x(m))
        xsend[t, 2] = (po[xrows(m), a:b] + xrecv[t, 0].astype(F32)).astype(BF)
        send(("o2", t), xsend.at[t, 2], xrecv.at[t, 2], at_x(m))

    def x_last(t, m):
        a, b = t * F, (t + 1) * F
        recv(("o1", t), xrecv.at[t, 1], at_x(-m))
        zs[:, a:b] = po[xrows(0), a:b] + xrecv[t, 1].astype(F32)
        recv(("o2", t), xrecv.at[t, 2], at_x(m))
        zs[:, a:b] += xrecv[t, 2].astype(F32)
        zsend[:, a:b] = zs[:, a:b].astype(BF)

    scale = 1.0 / math.sqrt(2 * R)
    WN = 2 * BLK

    def w_gu(gs, n):
        tk = slice(gs * R, gs * R + R)
        full = nn(xt[:, tk], hall[tk, HU + n : HU + n + WN])
        if gs == 0:
            acc_gu[:, n : n + WN] = full
            return
        full = ((full + acc_gu[:, n : n + WN]) * scale).astype(BF)
        for i in range(d.DB):
            for j in range(2):
                at = n // BLK + j
                dst, jj = (dg, at) if at < d.FB else (du, at - d.FB)
                dst[i * d.FB + jj] = full[i * BLK : (i + 1) * BLK, j * BLK : (j + 1) * BLK]

    def w_d(gs, n):
        tk = slice(gs * R, gs * R + R)
        full = nn(ht[:, tk], xr[1, tk, n : n + WN])
        if gs == 0:
            acc_d[:, n : n + WN] = full
            return
        full = ((full + acc_d[:, n : n + WN]) * scale).astype(BF)
        for i in range(d.FB):
            for j in range(2):
                dd[i * d.DB + n // BLK + j] = full[i * BLK : (i + 1) * BLK, j * BLK : (j + 1) * BLK]

    po[:, 0:F] = nn(hall[0:R, 0:HU], wd[...])
    x_first(0, 1)
    po[:, F : 2 * F] = nt(hall[0:R, HU:N], wgu[...])
    x_first(1, -1)
    ag_step(1, 1)
    steps = list(range(0, GU, WN))
    some = len(steps) // 2
    for n in steps[:some]:
        w_gu(0, n)
    x_second(0, 1)
    x_second(1, -1)
    ag_step(1, 2)
    for n in steps[some:]:
        w_gu(0, n)
    for s in range(3, d.LONG):
        ag_step(1, s)
    x_last(0, 1)
    x_last(1, -1)
    for o in range(1, d.Z):
        send(("oz", o), zsend.at[rows(zm(o) * T, T)], zrecv.at[o - 1], at_z(o))
    if d.LONG > 2:
        ag_step(1, d.LONG)
    ht[:, 0:R] = hall[0:R, 0:HU].T
    for n in range(0, F, WN):
        w_d(0, n)
    b_end(0)
    b_end(1)
    xt[:, R : 2 * R] = xr[0, R : 2 * R, :].T
    ag_partner(1)
    for buf in (dg, du, dd):
        buf[d.SL] = jnp.zeros((BLK, BLK), BF)

    def pick(ref, per, src, dst, out, sem):
        for s in range(d.CAP):
            at = ref[0, s] * per + ref[1, s]
            dst[s] = src[jnp.where(at < 0, jnp.int32(d.SL), at)]
        c = pltpu.make_async_copy(dst, out, sem)
        c.start()
        return c

    for n in steps:
        w_gu(1, n)
    outs = [pick(gi, d.FB, dg, pg, g_out, lsem.at[2]), pick(ui, d.FB, du, pu, u_out, lsem.at[3])]
    ht[:, R : 2 * R] = hall[R : 2 * R, 0:HU].T
    for n in range(0, F, WN):
        w_d(1, n)
    outs.append(pick(di, d.DB, dd, pd, d_out, lsem.at[4]))

    final = zs[rows(z * T, T), :]
    for o in range(1, d.Z):
        recv(("oz", o), zrecv.at[o - 1], at_z(o))
        final = final + zrecv[o - 1].astype(F32)
    fin[...] = final.astype(BF)
    outs.append(pltpu.make_async_copy(fin.at[:, 0:F], o_out, lsem.at[0]))
    outs.append(pltpu.make_async_copy(fin.at[:, F : 2 * F], ig_out, lsem.at[1]))
    outs[-1].start()
    outs[-2].start()
    for c in outs:
        c.wait()
    for c in sent:
        c.wait_send()


def pass_kernel(*refs):
    n = 5
    ins, outs, bufs, isem, osem = refs[:n], refs[n : 2 * n], refs[2 * n : 3 * n], refs[3 * n], refs[3 * n + 1]
    first = [pltpu.make_async_copy(ins[i], bufs[i], isem.at[i]) for i in range(n)]
    second = [pltpu.make_async_copy(bufs[i], outs[i], osem.at[i]) for i in range(n)]
    for c in first:
        c.start()
    for a, b in zip(first, second):
        a.wait()
        b.start()
    for c in second:
        c.wait()


def on_device(d, tokens, cotangent, gate_blocks, gate_index, up_blocks, up_index, down_blocks, down_index):
    T, F, HU, N, R = d.T, d.F, d.HU, d.N, d.R
    listings = [a[0, 0].T for a in (gate_index, up_index, down_index)]
    blocks = [a[0, 0] for a in (gate_blocks, up_blocks, down_blocks)]
    anyspace = pl.BlockSpec(memory_space=pl.ANY)
    smem = pl.BlockSpec(memory_space=pltpu.SMEM)
    V = pltpu.VMEM
    ZT = d.Z * T
    grads = jax.ShapeDtypeStruct((d.CAP, BLK, BLK), BF)
    act = jax.ShapeDtypeStruct((T, F), BF)
    shapes = [act, act, grads, grads, grads]
    results = pl.pallas_call(
        functools.partial(main_kernel, d),
        out_shape=shapes,
        in_specs=[smem] * 3 + [anyspace] * 5,
        out_specs=[anyspace] * 5,
        scratch_shapes=[
            pltpu.SMEM((3 * d.SL,), jnp.int32),
            *[V((d.CAP + 1, BLK, BLK), BF)] * 3,
            V((F, 2 * HU), BF),
            V((HU, F), BF),
            V((2, 2 * R, F), BF),
            V((2, R, F), BF),
            V((d.HALF, N), F32),
            V((d.HALF, N), F32),
            V((d.HALF, N), F32),
            V((d.LONG, T, N), BF),
            V((d.LONG, T, N), BF),
            V((d.SHORT, T, N), BF),
            V((d.SHORT, T, N), BF),
            V((T, N), F32),
            V((2 * R, N), BF),
            V((R, 2 * F), F32),
            V((2, 3, ZT, F), BF),
            V((2, 3, ZT, F), BF),
            V((ZT, 2 * F), F32),
            V((ZT, 2 * F), BF),
            V((d.Z - 1, T, 2 * F), BF),
            V((T, 2 * F), BF),
            V((F, 2 * R), BF),
            V((HU, 2 * R), BF),
            V((F, 2 * HU), F32),
            V((HU, F), F32),
            *[V((d.SL + 1, BLK, BLK), BF)] * 3,
            *[V((d.CAP, BLK, BLK), BF)] * 3,
            pltpu.SemaphoreType.DMA((5,)),
            pltpu.SemaphoreType.DMA((d.NSEM,)),
            pltpu.SemaphoreType.DMA((d.NSEM,)),
        ],
        compiler_params=pltpu.CompilerParams(
            collective_id=0, has_side_effects=True, vmem_limit_bytes=60 * 1024 * 1024
        ),
        name="ffn_main",
    )(*listings, tokens, cotangent, *blocks)
    o, ig, gg, ug, dgr = pl.pallas_call(
        pass_kernel,
        out_shape=shapes,
        in_specs=[anyspace] * 5,
        out_specs=[anyspace] * 5,
        scratch_shapes=[V(s.shape, BF) for s in shapes]
        + [pltpu.SemaphoreType.DMA((5,)), pltpu.SemaphoreType.DMA((5,))],
        compiler_params=pltpu.CompilerParams(vmem_limit_bytes=60 * 1024 * 1024),
        name="ffn_pass",
    )(*results)
    shape = gate_blocks.shape
    return (o, ig, gg.reshape(shape), ug.reshape(shape), dgr.reshape(shape))


def build(mesh, units):
    def body(tokens, cotangent, *rest):
        d = Dims(mesh.shape, tokens.shape[0], tokens.shape[1], rest[0].shape[2], units)
        return on_device(d, tokens, cotangent, *rest)

    act = P(("dp", "col"), "row")
    blocks = P("row", "col", None, None, None)
    index = P("row", "col", None, None)
    return jax.shard_map(
        body,
        mesh=mesh,
        in_specs=(act, act, blocks, index, blocks, index, blocks, index),
        out_specs=(act, act, blocks, blocks, blocks),
        check_vma=False,
    )


def solution(mesh):
    return build(mesh, 7)
```

```python
import functools
import math

import jax
import jax.numpy as jnp
from jax import lax
from jax.experimental import pallas as pl
from jax.experimental.pallas import tpu as pltpu
from jax.sharding import PartitionSpec as P

BLK = 128
XS = 4
MESH = pl.DeviceIdType.MESH
BF = jnp.bfloat16
F32 = jnp.float32


def split_tiles(tiles, parts, whole=False):
    cuts = [(tiles * i) // parts for i in range(parts + 1)]
    if whole:
        cuts = sorted({t * (tiles // 3) + c for t in range(3) for c in (0, (tiles // 3 + 1) // 2)} | {tiles})
        parts = len(cuts) - 1
    return [(cuts[i] * BLK, cuts[i + 1] * BLK, -1 if i % 2 == 0 else 1) for i in range(parts)]


class Dims:
    def __init__(self, mesh_shape, tok_rows, feat, cap, units):
        self.T = tok_rows
        self.F = feat
        self.CAP = cap
        self.DB = feat // BLK
        self.FB = units
        self.HU = units * BLK
        self.N = 3 * self.HU
        self.X = XS
        self.Z = mesh_shape["col"] // XS
        self.Y = mesh_shape["row"] // 2
        assert self.Y == 8 and self.X == 4
        self.NCOL = mesh_shape["col"]
        self.NROW = mesh_shape["row"]
        self.R = self.NCOL * self.T
        self.HALF = self.Y * self.T
        self.SL = self.DB * self.FB
        self.RS = split_tiles(3 * self.FB, 6, True)
        self.AG = split_tiles(3 * self.FB, 4)
        self.NSEM = 256


def main_kernel(
    d, gi, ui, di, tok, cot, gb, ub, db,
    o_out, ig_out, g_out, u_out, d_out,
    inv, wb0, wb1, wb2, wgu, wd, xr, xp, psend, precv, s1, rsend, rrecv, tot, hall,
    po, xsend, xrecv, zs, zsend, zrecv, fin, xt, ht, acc_gu, acc_d, dg, du, dd, pg, pu, pd,
    lsem, ssem, rsem,
):
    g = lax.axis_index("dp")
    row = lax.axis_index("row")
    col = lax.axis_index("col")
    y, k = lax.div(row, 2), lax.rem(row, 2)
    x, z = lax.div(col, d.Z), lax.rem(col, d.Z)
    T, F, HU, N, R = d.T, d.F, d.HU, d.N, d.R
    GU = 2 * HU
    ZT = d.Z * T
    wblk = (wb0, wb1, wb2)

    def ym(v):
        return lax.rem(y + v + 2 * d.Y, d.Y)

    def xm(v):
        return lax.rem(x + v + 2 * d.X, d.X)

    def zm(v):
        return lax.rem(z + v + 2 * d.Z, d.Z)

    def rows(start, size):
        return pl.ds(pl.multiple_of(start, size), size)

    def at_y(v):
        return {"row": ym(v) * 2 + k}

    def at_x(v):
        return {"col": xm(v) * d.Z + z}

    def at_z(v):
        return {"col": x * d.Z + zm(v)}

    def at_other_z(v):
        return {"dp": 1 - g, "col": x * d.Z + zm(v)}

    partner = {"row": y * 2 + 1 - k}

    sent = []
    ids = {}

    def number(name):
        if name not in ids:
            ids[name] = len(ids)
            assert len(ids) <= d.NSEM
        return ids[name]

    def send(name, src, dst, dev):
        i = number(name)
        c = pltpu.make_async_remote_copy(
            src_ref=src, dst_ref=dst, send_sem=ssem.at[i], recv_sem=rsem.at[i],
            device_id=dev, device_id_type=MESH,
        )
        c.start()
        sent.append(c)

    def recv(name, landing, dev):
        i = number(name)
        pltpu.make_async_remote_copy(
            src_ref=landing, dst_ref=landing, send_sem=ssem.at[i], recv_sem=rsem.at[i],
            device_id=dev, device_id_type=MESH,
        ).wait_recv()

    barrier = pltpu.get_barrier_semaphore()
    peers = [at_z(o) for o in range(1, d.Z)] + [at_other_z(o) for o in range(d.Z)]
    peers += [at_x(v) for v in range(1, d.X)] + [at_y(v) for v in (1, -1, 2, -2)] + [partner]
    for p in peers:
        pl.semaphore_signal(barrier, inc=1, device_id=p, device_id_type=MESH)

    own_rows = rows(col * T, T)
    loads = [
        pltpu.make_async_copy(tok, xr.at[0, own_rows], lsem.at[0]),
        pltpu.make_async_copy(cot, xr.at[1, own_rows], lsem.at[1]),
        pltpu.make_async_copy(gb, wb0.at[pl.ds(0, d.CAP)], lsem.at[2]),
        pltpu.make_async_copy(ub, wb1.at[pl.ds(0, d.CAP)], lsem.at[3]),
        pltpu.make_async_copy(db, wb2.at[pl.ds(0, d.CAP)], lsem.at[4]),
    ]
    for c in loads:
        c.start()

    pl.semaphore_wait(barrier, len(peers))

    def chunk(t, v, o):
        return xr.at[t, rows((xm(v) * d.Z + zm(-o)) * T, T)]

    def x_chunk(t, o, src):
        for v in (2, 1, -1):
            send(("xc", t, o, v), src, chunk(t, 0, o), at_x(v))

    def x_end(t, o):
        for v in (2, 1, -1):
            recv(("xc", t, o, v), chunk(t, -v, o), at_x(v))

    for t, src in ((0, tok), (1, cot)):
        for o in range(1, d.Z):
            send(("z0", t, o), src, xr.at[t, own_rows], at_z(o))
        x_chunk(t, 0, src)

    for t, (ref, per) in enumerate(((gi, d.FB), (ui, d.FB), (di, d.DB))):
        wblk[t][d.CAP] = jnp.zeros((BLK, BLK), BF)
        spots = [ref[0, s] * per + ref[1, s] for s in range(d.CAP)]

        def find(p, _, t=t, spots=spots):
            found = jnp.int32(d.CAP)
            for s in range(d.CAP):
                found = jnp.where(spots[s] == p, jnp.int32(s), found)
            inv[t * d.SL + p] = found
            return 0

        lax.fori_loop(0, d.SL, find, 0)

    def z_chunks(t):
        for o in range(1, d.Z):
            recv(("z0", t, o), chunk(t, 0, o), at_z(o))
            x_chunk(t, o, chunk(t, 0, o))

    def dense(t, per):
        loads[2 + t].wait()

        def put(p, _):
            i, j = lax.div(p, per), lax.rem(p, per)
            block = wblk[t][inv[t * d.SL + p]]
            if t < 2:
                wgu[rows(i * BLK, BLK), rows(j * BLK + t * HU, BLK)] = block
            else:
                wd[rows(i * BLK, BLK), rows(j * BLK, BLK)] = block
            return 0

        lax.fori_loop(0, d.SL, put, 0)

    z_chunks(0)
    z_chunks(1)

    other_rows = rows(R + col * T, T)
    for t, src in ((0, tok), (1, cot)):
        for o in range(d.Z):
            send(("z1", t, o), src, xr.at[t, other_rows], at_other_z(o))

    def z_other(t):
        for o in range(d.Z):
            recv(("z1", t, o), xr.at[t, rows(R + (x * d.Z + zm(-o)) * T, T)], at_z(o))

    def xblock(t, v):
        return xr.at[t, rows(R + xm(v) * ZT, ZT)]

    def b_send(t):
        for v in (2, 1, -1):
            send(("xb", t, v), xblock(t, 0), xblock(t, 0), at_x(v))

    def b_end(t):
        for v in (2, 1, -1):
            recv(("xb", t, v), xblock(t, -v), at_x(v))

    dense(0, d.FB)
    dense(1, d.FB)
    dense(2, d.DB)
    loads[0].wait()
    loads[1].wait()
    for t in (0, 1):
        for o in range(d.Z):
            x_end(t, o)

    def nt(a, b):
        return lax.dot_general(a, b, (((1,), (1,)), ((), ())), preferred_element_type=F32)

    def nn(a, b):
        return jnp.dot(a, b, preferred_element_type=F32)

    H = d.HALF
    for t in (0, 1):
        xp[t, 0:H] = xr[t, rows((1 - k) * H, H), :]
        xp[t, H : 2 * H] = xr[t, rows(k * H, H), :]
    for q, (a, b, _) in enumerate(d.RS):
        part = nn(xp[0], wgu[:, a:b]) if b <= GU else nt(xp[1], wd[a - GU : b - GU, :])
        psend[:, a:b] = part[0:H].astype(BF)
        send(("p", q), psend.at[:, a:b], precv.at[:, a:b], partner)
        s1[:, a:b] = part[H : 2 * H]

    def rs_first(slot, q, m, far, hop):
        a, b, _ = d.RS[q]
        rsend[slot, :, a:b] = s1[rows(ym(m * far) * T, T), a:b].astype(BF)
        send(("r", slot, q), rsend.at[slot, :, a:b], rrecv.at[slot, :, a:b], at_y(m * hop))

    def rs_got(slot, q, m, hop):
        a, b, _ = d.RS[q]
        recv(("r", slot, q), rrecv.at[slot, :, a:b], at_y(m * hop))
        return rrecv[slot, :, a:b].astype(F32)

    for q, (a, b, m) in enumerate(d.RS):
        recv(("p", q), precv.at[:, a:b], partner)
        s1[:, a:b] += precv[:, a:b].astype(F32)
        rs_first(0, q, m, 4, 2)
        rs_first(1, q, m, 3, 1)
        rs_first(4, q, -m, 3, 1)
        rs_first(3, q, m, 1, 1)
        rs_first(6, q, -m, 1, 1)
    for q, (a, b, m) in enumerate(d.RS):
        full = s1[rows(ym(2 * m) * T, T), a:b] + rs_got(0, q, m, 2) + rs_got(1, q, m, 1)
        rsend[2, :, a:b] = full.astype(BF)
        send(("r", 2, q), rsend.at[2, :, a:b], rrecv.at[2, :, a:b], at_y(2 * m))
        full = s1[rows(ym(-2 * m) * T, T), a:b] + rs_got(4, q, -m, 1)
        rsend[5, :, a:b] = full.astype(BF)
        send(("r", 5, q), rsend.at[5, :, a:b], rrecv.at[5, :, a:b], at_y(-2 * m))
    for t in (0, 1):
        z_other(t)
        b_send(t)
    xt[:, 0:R] = xr[0, 0:R, :].T
    for q, (a, b, m) in enumerate(d.RS):
        full = s1[rows(y * T, T), a:b] + rs_got(3, q, m, 1) + rs_got(6, q, -m, 1)
        tot[:, a:b] = full + rs_got(2, q, m, 2) + rs_got(5, q, -m, 2)

    gate, up, gh = tot[:, 0:HU], tot[:, HU:GU], tot[:, GU:N]
    sig = jax.nn.sigmoid(gate)
    mine_rows = rows((k * d.Y + y) * T, T)
    hall[mine_rows, 0:HU] = (gate * sig * up).astype(BF)
    hall[mine_rows, HU:GU] = (gh * up * sig * (1.0 + gate * (1.0 - sig))).astype(BF)
    hall[mine_rows, GU:N] = (gh * gate * sig).astype(BF)

    def hrows(gs, kk, yy):
        return rows(gs * R + (kk * d.Y + yy) * T, T)

    def ag_ref(gs, v, q):
        a, b, _ = d.AG[q]
        return hall.at[hrows(gs, k, ym(v)), a:b]

    def ag_send(gs, q, m, src, dst):
        ref = ag_ref(gs, -m * src, q)
        send(("a", gs, q, m * dst), ref, ref, at_y(m * (dst - src)))

    def ag_recv(gs, q, m, dst):
        recv(("a", gs, q, m * dst), ag_ref(gs, -m * dst, q), at_y(m))

    def to_partner(gs, v):
        ref = hall.at[hrows(gs, k, ym(v))]
        send(("ap", gs, v), ref, ref, partner)

    def ag_start(gs):
        for dst in (2, 1):
            for q, (_, _, m) in enumerate(d.AG):
                ag_send(gs, q, m, 0, dst)
                ag_send(gs, q, -m, 0, dst)
        to_partner(gs, 0)

    def ag_step(gs):
        for q, (_, _, m) in enumerate(d.AG):
            ag_recv(gs, q, m, 2)
            ag_send(gs, q, m, 2, 3)
            ag_send(gs, q, m, 2, 4)
            ag_recv(gs, q, -m, 2)
            ag_send(gs, q, -m, 2, 3)
        for v in (2, -2):
            to_partner(gs, v)
        for q in range(len(d.AG)):
            ag_recv(gs, q, 1, 1)
            ag_recv(gs, q, -1, 1)
        for v in (1, -1):
            to_partner(gs, v)

    def ag_last(gs):
        for q in range(len(d.AG)):
            ag_recv(gs, q, 1, 3)
            ag_recv(gs, q, -1, 3)
        for v in (3, -3):
            to_partner(gs, v)
        for q, (_, _, m) in enumerate(d.AG):
            ag_recv(gs, q, m, 4)
        to_partner(gs, 4)

    def ag_partner(gs):
        for v in range(-3, 5):
            recv(("ap", gs, v), hall.at[hrows(gs, 1 - k, ym(v))], partner)

    ag_start(0)
    send("dp", hall.at[mine_rows], hall.at[hrows(1, k, y)], {"dp": 1 - g})
    ag_step(0)
    ag_last(0)
    recv("dp", hall.at[hrows(1, k, y)], {"dp": 1 - g})
    ag_start(1)

    def xrows(v):
        return rows(xm(v) * ZT, ZT)

    FAR = (2, 1, -1)

    def x_copy(t, i):
        return pltpu.make_async_remote_copy(
            src_ref=xsend.at[t, i], dst_ref=xrecv.at[t, i], send_sem=ssem.at[number(("ox", t, i))],
            recv_sem=rsem.at[number(("ox", t, i))], device_id=at_x(FAR[i]), device_id_type=MESH,
        )

    def x_first(t, half):
        for i, v in enumerate(FAR):

            @pl.when(lax.div(xm(v), d.X // 2) == half)
            def _(i=i, v=v):
                xsend[t, i] = po[xrows(v), t * F : (t + 1) * F].astype(BF)
                x_copy(t, i).start()

    def x_last(t):
        a, b = t * F, (t + 1) * F
        full = po[xrows(0), a:b]
        for i, v in enumerate(FAR):
            recv(("ox", t, i), xrecv.at[t, i], at_x(v))
            full = full + xrecv[t, i].astype(F32)
        zs[:, a:b] = full
        zsend[t] = full.astype(BF)
        for o in range(1, d.Z):
            send(("oz", t, o), zsend.at[t, rows(zm(o) * T, T)], zrecv.at[t, o - 1], at_z(o))

    scale = 1.0 / math.sqrt(2 * R)
    WN = 2 * BLK

    def w_gu(gs, n):
        tk = slice(gs * R, gs * R + R)
        full = nn(xt[:, tk], hall[tk, HU + n : HU + n + WN])
        if gs == 0:
            acc_gu[:, n : n + WN] = full
            return
        full = ((full + acc_gu[:, n : n + WN]) * scale).astype(BF)
        for i in range(d.DB):
            for j in range(2):
                at = n // BLK + j
                dst, jj = (dg, at) if at < d.FB else (du, at - d.FB)
                dst[i * d.FB + jj] = full[i * BLK : (i + 1) * BLK, j * BLK : (j + 1) * BLK]

    def w_d(gs, n):
        tk = slice(gs * R, gs * R + R)
        full = nn(ht[:, tk], xr[1, tk, n : n + WN])
        if gs == 0:
            acc_d[:, n : n + WN] = full
            return
        full = ((full + acc_d[:, n : n + WN]) * scale).astype(BF)
        for i in range(d.FB):
            for j in range(2):
                dd[i * d.DB + n // BLK + j] = full[i * BLK : (i + 1) * BLK, j * BLK : (j + 1) * BLK]

    for half in (k, 1 - k):
        rh = rows(half * H, H)
        po[rh, 0:F] = nn(hall[rh, 0:HU], wd[...])
        x_first(0, half)
        po[rh, F : 2 * F] = nt(hall[rh, HU:N], wgu[...])
        x_first(1, half)
        if half is k:
            ag_partner(0)
    for t in (0, 1):
        for i in range(len(FAR)):
            sent.append(x_copy(t, i))
    steps = list(range(0, GU, WN))
    for n in steps:
        w_gu(0, n)
    ht[:, 0:R] = hall[0:R, 0:HU].T
    for n in range(0, F, WN):
        w_d(0, n)
    ag_step(1)
    x_last(0)
    x_last(1)
    ag_last(1)
    b_end(0)
    b_end(1)
    xt[:, R : 2 * R] = xr[0, R : 2 * R, :].T
    ag_partner(1)
    for buf in (dg, du, dd):
        buf[d.SL] = jnp.zeros((BLK, BLK), BF)

    def pick(ref, per, src, dst, out, sem):
        for s in range(d.CAP):
            at = ref[0, s] * per + ref[1, s]
            dst[s] = src[jnp.where(at < 0, jnp.int32(d.SL), at)]
        c = pltpu.make_async_copy(dst, out, sem)
        c.start()
        return c

    for n in steps:
        w_gu(1, n)
    outs = [pick(gi, d.FB, dg, pg, g_out, lsem.at[2]), pick(ui, d.FB, du, pu, u_out, lsem.at[3])]
    ht[:, R : 2 * R] = hall[R : 2 * R, 0:HU].T
    for n in range(0, F, WN):
        w_d(1, n)
    outs.append(pick(di, d.DB, dd, pd, d_out, lsem.at[4]))

    for t in (0, 1):
        full = zs[rows(z * T, T), t * F : (t + 1) * F]
        for o in range(1, d.Z):
            recv(("oz", t, o), zrecv.at[t, o - 1], at_z(o))
            full = full + zrecv[t, o - 1].astype(F32)
        fin[:, t * F : (t + 1) * F] = full.astype(BF)
    outs.append(pltpu.make_async_copy(fin.at[:, 0:F], o_out, lsem.at[0]))
    outs.append(pltpu.make_async_copy(fin.at[:, F : 2 * F], ig_out, lsem.at[1]))
    outs[-1].start()
    outs[-2].start()
    for c in outs:
        c.wait()
    for c in sent:
        c.wait_send()


def pass_kernel(*refs):
    n = 5
    ins, outs, bufs, isem, osem = refs[:n], refs[n : 2 * n], refs[2 * n : 3 * n], refs[3 * n], refs[3 * n + 1]
    first = [pltpu.make_async_copy(ins[i], bufs[i], isem.at[i]) for i in range(n)]
    second = [pltpu.make_async_copy(bufs[i], outs[i], osem.at[i]) for i in range(n)]
    for c in first:
        c.start()
    for a, b in zip(first, second):
        a.wait()
        b.start()
    for c in second:
        c.wait()


def on_device(d, tokens, cotangent, gate_blocks, gate_index, up_blocks, up_index, down_blocks, down_index):
    T, F, HU, N, R = d.T, d.F, d.HU, d.N, d.R
    listings = [a[0, 0].T for a in (gate_index, up_index, down_index)]
    blocks = [a[0, 0] for a in (gate_blocks, up_blocks, down_blocks)]
    anyspace = pl.BlockSpec(memory_space=pl.ANY)
    smem = pl.BlockSpec(memory_space=pltpu.SMEM)
    V = pltpu.VMEM
    ZT = d.Z * T
    grads = jax.ShapeDtypeStruct((d.CAP, BLK, BLK), BF)
    act = jax.ShapeDtypeStruct((T, F), BF)
    shapes = [act, act, grads, grads, grads]
    results = pl.pallas_call(
        functools.partial(main_kernel, d),
        out_shape=shapes,
        in_specs=[smem] * 3 + [anyspace] * 5,
        out_specs=[anyspace] * 5,
        scratch_shapes=[
            pltpu.SMEM((3 * d.SL,), jnp.int32),
            *[V((d.CAP + 1, BLK, BLK), BF)] * 3,
            V((F, 2 * HU), BF),
            V((HU, F), BF),
            V((2, 2 * R, F), BF),
            V((2, R, F), BF),
            V((d.HALF, N), BF),
            V((d.HALF, N), BF),
            V((d.HALF, N), F32),
            V((7, T, N), BF),
            V((7, T, N), BF),
            V((T, N), F32),
            V((2 * R, N), BF),
            V((R, 2 * F), F32),
            V((2, 3, ZT, F), BF),
            V((2, 3, ZT, F), BF),
            V((ZT, 2 * F), F32),
            V((2, ZT, F), BF),
            V((2, d.Z - 1, T, F), BF),
            V((T, 2 * F), BF),
            V((F, 2 * R), BF),
            V((HU, 2 * R), BF),
            V((F, 2 * HU), F32),
            V((HU, F), F32),
            *[V((d.SL + 1, BLK, BLK), BF)] * 3,
            *[V((d.CAP, BLK, BLK), BF)] * 3,
            pltpu.SemaphoreType.DMA((5,)),
            pltpu.SemaphoreType.DMA((d.NSEM,)),
            pltpu.SemaphoreType.DMA((d.NSEM,)),
        ],
        compiler_params=pltpu.CompilerParams(
            collective_id=0, has_side_effects=True, vmem_limit_bytes=60 * 1024 * 1024
        ),
        name="ffn_main",
    )(*listings, tokens, cotangent, *blocks)
    o, ig, gg, ug, dgr = pl.pallas_call(
        pass_kernel,
        out_shape=shapes,
        in_specs=[anyspace] * 5,
        out_specs=[anyspace] * 5,
        scratch_shapes=[V(s.shape, BF) for s in shapes]
        + [pltpu.SemaphoreType.DMA((5,)), pltpu.SemaphoreType.DMA((5,))],
        compiler_params=pltpu.CompilerParams(vmem_limit_bytes=60 * 1024 * 1024),
        name="ffn_pass",
    )(*results)
    shape = gate_blocks.shape
    return (o, ig, gg.reshape(shape), ug.reshape(shape), dgr.reshape(shape))


def build(mesh, units):
    def body(tokens, cotangent, *rest):
        d = Dims(mesh.shape, tokens.shape[0], tokens.shape[1], rest[0].shape[2], units)
        return on_device(d, tokens, cotangent, *rest)

    act = P(("dp", "col"), "row")
    blocks = P("row", "col", None, None, None)
    index = P("row", "col", None, None)
    return jax.shard_map(
        body,
        mesh=mesh,
        in_specs=(act, act, blocks, index, blocks, index, blocks, index),
        out_specs=(act, act, blocks, blocks, blocks),
        check_vma=False,
    )


def solution(mesh):
    return build(mesh, 7)
```

```python
import functools
import math

import jax
import jax.numpy as jnp
from jax import lax
from jax.experimental import pallas as pl
from jax.experimental.pallas import tpu as pltpu
from jax.sharding import PartitionSpec as P

BLK = 128
XS = 4
MESH = pl.DeviceIdType.MESH
BF = jnp.bfloat16
F32 = jnp.float32


def split_tiles(tiles, parts, whole=False):
    cuts = [(tiles * i) // parts for i in range(parts + 1)]
    if whole:
        cuts = sorted({t * (tiles // 3) + c for t in range(3) for c in (0, (tiles // 3 + 1) // 2)} | {tiles})
        parts = len(cuts) - 1
    return [(cuts[i] * BLK, cuts[i + 1] * BLK, -1 if i % 2 == 0 else 1) for i in range(parts)]


class Dims:
    def __init__(self, mesh_shape, tok_rows, feat, cap, units):
        self.T = tok_rows
        self.F = feat
        self.CAP = cap
        self.DB = feat // BLK
        self.FB = units
        self.HU = units * BLK
        self.N = 3 * self.HU
        self.X = XS
        self.Z = mesh_shape["col"] // XS
        self.Y = mesh_shape["row"] // 2
        assert self.Y == 8 and self.X == 4
        self.NCOL = mesh_shape["col"]
        self.NROW = mesh_shape["row"]
        self.R = self.NCOL * self.T
        self.HALF = self.Y * self.T
        self.SL = self.DB * self.FB
        self.RS = split_tiles(3 * self.FB, 6, True)
        h, c = self.HU, (self.FB + 1) // 2 * BLK
        self.AG = [[(0, c, -1), (c, h, 1)], [(h, 2 * h, -1), (2 * h, 3 * h, 1)]]
        self.NSEM = 256


def main_kernel(
    d, gi, ui, di, tok, cot, gb, ub, db,
    o_out, ig_out, g_out, u_out, d_out,
    inv, wb0, wb1, wb2, wgu, wd, xr, xp, psend, precv, s1, rsend, rrecv, tot, hall,
    po, xsend, xrecv, zs, zsend, zrecv, fin, xt, ht, acc_gu, acc_d, dg, du, dd, pg, pu, pd,
    lsem, ssem, rsem,
):
    g = lax.axis_index("dp")
    row = lax.axis_index("row")
    col = lax.axis_index("col")
    y, k = lax.div(row, 2), lax.rem(row, 2)
    x, z = lax.div(col, d.Z), lax.rem(col, d.Z)
    T, F, HU, N, R = d.T, d.F, d.HU, d.N, d.R
    GU = 2 * HU
    ZT = d.Z * T
    wblk = (wb0, wb1, wb2)

    def ym(v):
        return lax.rem(y + v + 2 * d.Y, d.Y)

    def xm(v):
        return lax.rem(x + v + 2 * d.X, d.X)

    def zm(v):
        return lax.rem(z + v + 2 * d.Z, d.Z)

    def rows(start, size):
        return pl.ds(pl.multiple_of(start, size), size)

    def at_y(v):
        return {"row": ym(v) * 2 + k}

    def at_x(v):
        return {"col": xm(v) * d.Z + z}

    def at_z(v):
        return {"col": x * d.Z + zm(v)}

    def at_other_z(v):
        return {"dp": 1 - g, "col": x * d.Z + zm(v)}

    partner = {"row": y * 2 + 1 - k}

    sent = []
    ids = {}

    def number(name):
        if name not in ids:
            ids[name] = len(ids)
            assert len(ids) <= d.NSEM
        return ids[name]

    def send(name, src, dst, dev):
        i = number(name)
        c = pltpu.make_async_remote_copy(
            src_ref=src, dst_ref=dst, send_sem=ssem.at[i], recv_sem=rsem.at[i],
            device_id=dev, device_id_type=MESH,
        )
        c.start()
        sent.append(c)

    def recv(name, landing, dev):
        i = number(name)
        pltpu.make_async_remote_copy(
            src_ref=landing, dst_ref=landing, send_sem=ssem.at[i], recv_sem=rsem.at[i],
            device_id=dev, device_id_type=MESH,
        ).wait_recv()

    barrier = pltpu.get_barrier_semaphore()
    peers = [at_z(o) for o in range(1, d.Z)] + [at_other_z(o) for o in range(d.Z)]
    peers += [at_x(v) for v in range(1, d.X)] + [at_y(v) for v in (1, -1, 2, -2)] + [partner]
    for p in peers:
        pl.semaphore_signal(barrier, inc=1, device_id=p, device_id_type=MESH)

    own_rows = rows(col * T, T)
    loads = [
        pltpu.make_async_copy(tok, xr.at[0, own_rows], lsem.at[0]),
        pltpu.make_async_copy(cot, xr.at[1, own_rows], lsem.at[1]),
        pltpu.make_async_copy(gb, wb0.at[pl.ds(0, d.CAP)], lsem.at[2]),
        pltpu.make_async_copy(ub, wb1.at[pl.ds(0, d.CAP)], lsem.at[3]),
        pltpu.make_async_copy(db, wb2.at[pl.ds(0, d.CAP)], lsem.at[4]),
    ]
    for c in loads:
        c.start()

    pl.semaphore_wait(barrier, len(peers))

    def chunk(t, v, o):
        return xr.at[t, rows((xm(v) * d.Z + zm(-o)) * T, T)]

    def x_chunk(t, o, src):
        for v in (2, 1, -1):
            send(("xc", t, o, v), src, chunk(t, 0, o), at_x(v))

    def x_end(t, o):
        for v in (2, 1, -1):
            recv(("xc", t, o, v), chunk(t, -v, o), at_x(v))

    for t, src in ((0, tok), (1, cot)):
        for o in range(1, d.Z):
            send(("z0", t, o), src, xr.at[t, own_rows], at_z(o))
        x_chunk(t, 0, src)

    for t, (ref, per) in enumerate(((gi, d.FB), (ui, d.FB), (di, d.DB))):
        wblk[t][d.CAP] = jnp.zeros((BLK, BLK), BF)
        spots = [ref[0, s] * per + ref[1, s] for s in range(d.CAP)]

        def find(p, _, t=t, spots=spots):
            found = jnp.int32(d.CAP)
            for s in range(d.CAP):
                found = jnp.where(spots[s] == p, jnp.int32(s), found)
            inv[t * d.SL + p] = found
            return 0

        lax.fori_loop(0, d.SL, find, 0)

    def z_chunks(t):
        for o in range(1, d.Z):
            recv(("z0", t, o), chunk(t, 0, o), at_z(o))
            x_chunk(t, o, chunk(t, 0, o))

    def dense(t, per):
        loads[2 + t].wait()

        def put(p, _):
            i, j = lax.div(p, per), lax.rem(p, per)
            block = wblk[t][inv[t * d.SL + p]]
            if t < 2:
                wgu[rows(i * BLK, BLK), rows(j * BLK + t * HU, BLK)] = block
            else:
                wd[rows(i * BLK, BLK), rows(j * BLK, BLK)] = block
            return 0

        lax.fori_loop(0, d.SL, put, 0)

    z_chunks(0)
    z_chunks(1)

    other_rows = rows(R + col * T, T)
    for t, src in ((0, tok), (1, cot)):
        for o in range(d.Z):
            send(("z1", t, o), src, xr.at[t, other_rows], at_other_z(o))

    def z_other(t):
        for o in range(d.Z):
            recv(("z1", t, o), xr.at[t, rows(R + (x * d.Z + zm(-o)) * T, T)], at_z(o))

    def xblock(t, v):
        return xr.at[t, rows(R + xm(v) * ZT, ZT)]

    def b_send(t):
        for v in (2, 1, -1):
            send(("xb", t, v), xblock(t, 0), xblock(t, 0), at_x(v))

    def b_end(t):
        for v in (2, 1, -1):
            recv(("xb", t, v), xblock(t, -v), at_x(v))

    dense(0, d.FB)
    dense(1, d.FB)
    dense(2, d.DB)
    loads[0].wait()
    loads[1].wait()

    def nt(a, b):
        return lax.dot_general(a, b, (((1,), (1,)), ((), ())), preferred_element_type=F32)

    def nn(a, b):
        return jnp.dot(a, b, preferred_element_type=F32)

    H = d.HALF

    def halves(t):
        for o in range(d.Z):
            x_end(t, o)
        xp[t, 0:H] = xr[t, rows((1 - k) * H, H), :]
        xp[t, H : 2 * H] = xr[t, rows(k * H, H), :]

    def partial(q):
        a, b, _ = d.RS[q]
        part = nn(xp[0], wgu[:, a:b]) if b <= GU else nt(xp[1], wd[a - GU : b - GU, :])
        psend[:, a:b] = part[0:H].astype(BF)
        send(("p", q), psend.at[:, a:b], precv.at[:, a:b], partner)
        s1[:, a:b] = part[H : 2 * H]

    def rs_first(slot, q, m, far, hop):
        a, b, _ = d.RS[q]
        rsend[slot, :, a:b] = s1[rows(ym(m * far) * T, T), a:b].astype(BF)
        send(("r", slot, q), rsend.at[slot, :, a:b], rrecv.at[slot, :, a:b], at_y(m * hop))

    def rs_got(slot, q, m, hop):
        a, b, _ = d.RS[q]
        recv(("r", slot, q), rrecv.at[slot, :, a:b], at_y(m * hop))
        return rrecv[slot, :, a:b].astype(F32)

    def rs_start(q):
        a, b, m = d.RS[q]
        recv(("p", q), precv.at[:, a:b], partner)
        s1[:, a:b] += precv[:, a:b].astype(F32)
        rs_first(0, q, m, 4, 2)
        rs_first(1, q, m, 3, 1)
        rs_first(4, q, -m, 3, 1)
        rs_first(3, q, m, 1, 1)
        rs_first(6, q, -m, 1, 1)

    def rs_second(q):
        a, b, m = d.RS[q]
        full = s1[rows(ym(2 * m) * T, T), a:b] + rs_got(0, q, m, 2) + rs_got(1, q, m, 1)
        rsend[2, :, a:b] = full.astype(BF)
        send(("r", 2, q), rsend.at[2, :, a:b], rrecv.at[2, :, a:b], at_y(2 * m))
        full = s1[rows(ym(-2 * m) * T, T), a:b] + rs_got(4, q, -m, 1)
        rsend[5, :, a:b] = full.astype(BF)
        send(("r", 5, q), rsend.at[5, :, a:b], rrecv.at[5, :, a:b], at_y(-2 * m))

    def rs_end(q):
        a, b, m = d.RS[q]
        full = s1[rows(y * T, T), a:b] + rs_got(3, q, m, 1) + rs_got(6, q, -m, 1)
        tot[:, a:b] = full + rs_got(2, q, m, 2) + rs_got(5, q, -m, 2)

    early = [q for q, (_, b, _) in enumerate(d.RS) if b <= GU]
    late = [q for q, (_, b, _) in enumerate(d.RS) if b > GU]
    for t, part in ((0, early), (1, late)):
        halves(t)
        for q in part:
            partial(q)
        for q in part:
            rs_start(q)
    for q in early + late:
        rs_second(q)
    for t in (0, 1):
        z_other(t)
        b_send(t)
    xt[:, 0:R] = xr[0, 0:R, :].T

    def hrows(gs, kk, yy):
        return rows(gs * R + (kk * d.Y + yy) * T, T)

    def ag_ref(gs, v, c):
        return hall.at[hrows(gs, k, ym(v)), c[0] : c[1]]

    def ag_send(gs, c, m, src, dst):
        ref = ag_ref(gs, -m * src, c)
        send(("a", gs, c[0], m * dst), ref, ref, at_y(m * (dst - src)))

    def ag_recv(gs, c, m, dst):
        recv(("a", gs, c[0], m * dst), ag_ref(gs, -m * dst, c), at_y(m))

    def to_partner(gs, grp, v):
        ref = ag_ref(gs, v, (d.AG[grp][0][0], d.AG[grp][-1][1]))
        send(("ap", gs, grp, v), ref, ref, partner)

    def ag_start(gs, grp):
        for dst in (2, 1):
            for c in d.AG[grp]:
                ag_send(gs, c, c[2], 0, dst)
                ag_send(gs, c, -c[2], 0, dst)
        to_partner(gs, grp, 0)

    def ag_step(gs, grp):
        for c in d.AG[grp]:
            m = c[2]
            ag_recv(gs, c, m, 2)
            ag_send(gs, c, m, 2, 3)
            ag_send(gs, c, m, 2, 4)
            ag_recv(gs, c, -m, 2)
            ag_send(gs, c, -m, 2, 3)
        for v in (2, -2):
            to_partner(gs, grp, v)
        for c in d.AG[grp]:
            ag_recv(gs, c, 1, 1)
            ag_recv(gs, c, -1, 1)
        for v in (1, -1):
            to_partner(gs, grp, v)

    def ag_last(gs, grp):
        for c in d.AG[grp]:
            ag_recv(gs, c, 1, 3)
            ag_recv(gs, c, -1, 3)
        for v in (3, -3):
            to_partner(gs, grp, v)
        for c in d.AG[grp]:
            ag_recv(gs, c, c[2], 4)
        to_partner(gs, grp, 4)

    def ag_partner(gs, grp):
        a, b = d.AG[grp][0][0], d.AG[grp][-1][1]
        for v in range(-3, 5):
            recv(("ap", gs, grp, v), hall.at[hrows(gs, 1 - k, ym(v)), a:b], partner)

    mine_rows = rows((k * d.Y + y) * T, T)
    for q in early:
        rs_end(q)
    gate, up = tot[:, 0:HU], tot[:, HU:GU]
    sig = jax.nn.sigmoid(gate)
    hall[mine_rows, 0:HU] = (gate * sig * up).astype(BF)
    ag_start(0, 0)
    for q in late:
        rs_end(q)
    gate, up, gh = tot[:, 0:HU], tot[:, HU:GU], tot[:, GU:N]
    sig = jax.nn.sigmoid(gate)
    hall[mine_rows, HU:GU] = (gh * up * sig * (1.0 + gate * (1.0 - sig))).astype(BF)
    hall[mine_rows, GU:N] = (gh * gate * sig).astype(BF)
    ag_start(0, 1)
    send("dp", hall.at[mine_rows], hall.at[hrows(1, k, y)], {"dp": 1 - g})
    ag_step(0, 0)
    ag_step(0, 1)
    ag_last(0, 0)

    def xrows(v):
        return rows(xm(v) * ZT, ZT)

    FAR = (2, 1, -1)

    def x_copy(t, i):
        return pltpu.make_async_remote_copy(
            src_ref=xsend.at[t, i], dst_ref=xrecv.at[t, i], send_sem=ssem.at[number(("ox", t, i))],
            recv_sem=rsem.at[number(("ox", t, i))], device_id=at_x(FAR[i]), device_id_type=MESH,
        )

    def x_first(t, half):
        for i, v in enumerate(FAR):

            @pl.when(lax.div(xm(v), d.X // 2) == half)
            def _(i=i, v=v):
                xsend[t, i] = po[xrows(v), t * F : (t + 1) * F].astype(BF)
                x_copy(t, i).start()

    def x_last(t):
        a, b = t * F, (t + 1) * F
        full = po[xrows(0), a:b]
        for i, v in enumerate(FAR):
            recv(("ox", t, i), xrecv.at[t, i], at_x(v))
            full = full + xrecv[t, i].astype(F32)
        zs[:, a:b] = full
        zsend[t] = full.astype(BF)
        for o in range(1, d.Z):
            send(("oz", t, o), zsend.at[t, rows(zm(o) * T, T)], zrecv.at[t, o - 1], at_z(o))

    scale = 1.0 / math.sqrt(2 * R)
    WN = 2 * BLK

    def w_gu(gs, n):
        tk = slice(gs * R, gs * R + R)
        full = nn(xt[:, tk], hall[tk, HU + n : HU + n + WN])
        if gs == 0:
            acc_gu[:, n : n + WN] = full
            return
        full = ((full + acc_gu[:, n : n + WN]) * scale).astype(BF)
        for i in range(d.DB):
            for j in range(2):
                at = n // BLK + j
                dst, jj = (dg, at) if at < d.FB else (du, at - d.FB)
                dst[i * d.FB + jj] = full[i * BLK : (i + 1) * BLK, j * BLK : (j + 1) * BLK]

    def w_d(gs, n):
        tk = slice(gs * R, gs * R + R)
        full = nn(ht[:, tk], xr[1, tk, n : n + WN])
        if gs == 0:
            acc_d[:, n : n + WN] = full
            return
        full = ((full + acc_d[:, n : n + WN]) * scale).astype(BF)
        for i in range(d.FB):
            for j in range(2):
                dd[i * d.DB + n // BLK + j] = full[i * BLK : (i + 1) * BLK, j * BLK : (j + 1) * BLK]

    def o_half(half):
        rh = rows(half * H, H)
        po[rh, 0:F] = nn(hall[rh, 0:HU], wd[...])
        x_first(0, half)

    def ig_half(half):
        rh = rows(half * H, H)
        po[rh, F : 2 * F] = nt(hall[rh, HU:N], wgu[...])
        x_first(1, half)

    o_half(k)
    ag_partner(0, 0)
    o_half(1 - k)
    ag_last(0, 1)
    ig_half(k)
    recv("dp", hall.at[hrows(1, k, y)], {"dp": 1 - g})
    ag_start(1, 0)
    ag_start(1, 1)
    ag_partner(0, 1)
    ig_half(1 - k)
    for t in (0, 1):
        for i in range(len(FAR)):
            sent.append(x_copy(t, i))
    steps = list(range(0, GU, WN))
    for n in steps:
        w_gu(0, n)
    ht[:, 0:R] = hall[0:R, 0:HU].T
    for n in range(0, F, WN):
        w_d(0, n)
    x_last(0)
    ag_step(1, 0)
    ag_step(1, 1)
    x_last(1)
    ag_last(1, 0)
    ag_last(1, 1)
    b_end(0)
    b_end(1)
    xt[:, R : 2 * R] = xr[0, R : 2 * R, :].T
    ag_partner(1, 0)
    ag_partner(1, 1)
    for buf in (dg, du, dd):
        buf[d.SL] = jnp.zeros((BLK, BLK), BF)

    def pick(ref, per, src, dst, out, sem):
        for s in range(d.CAP):
            at = ref[0, s] * per + ref[1, s]
            dst[s] = src[jnp.where(at < 0, jnp.int32(d.SL), at)]
        c = pltpu.make_async_copy(dst, out, sem)
        c.start()
        return c

    for n in steps:
        w_gu(1, n)
    outs = [pick(gi, d.FB, dg, pg, g_out, lsem.at[2]), pick(ui, d.FB, du, pu, u_out, lsem.at[3])]
    ht[:, R : 2 * R] = hall[R : 2 * R, 0:HU].T
    for n in range(0, F, WN):
        w_d(1, n)
    outs.append(pick(di, d.DB, dd, pd, d_out, lsem.at[4]))

    for t in (0, 1):
        full = zs[rows(z * T, T), t * F : (t + 1) * F]
        for o in range(1, d.Z):
            recv(("oz", t, o), zrecv.at[t, o - 1], at_z(o))
            full = full + zrecv[t, o - 1].astype(F32)
        fin[:, t * F : (t + 1) * F] = full.astype(BF)
    outs.append(pltpu.make_async_copy(fin.at[:, 0:F], o_out, lsem.at[0]))
    outs.append(pltpu.make_async_copy(fin.at[:, F : 2 * F], ig_out, lsem.at[1]))
    outs[-1].start()
    outs[-2].start()
    for c in outs:
        c.wait()
    for c in sent:
        c.wait_send()


def pass_kernel(*refs):
    n = 5
    ins, outs, bufs, isem, osem = refs[:n], refs[n : 2 * n], refs[2 * n : 3 * n], refs[3 * n], refs[3 * n + 1]
    first = [pltpu.make_async_copy(ins[i], bufs[i], isem.at[i]) for i in range(n)]
    second = [pltpu.make_async_copy(bufs[i], outs[i], osem.at[i]) for i in range(n)]
    for c in first:
        c.start()
    for a, b in zip(first, second):
        a.wait()
        b.start()
    for c in second:
        c.wait()


def on_device(d, tokens, cotangent, gate_blocks, gate_index, up_blocks, up_index, down_blocks, down_index):
    T, F, HU, N, R = d.T, d.F, d.HU, d.N, d.R
    listings = [a[0, 0].T for a in (gate_index, up_index, down_index)]
    blocks = [a[0, 0] for a in (gate_blocks, up_blocks, down_blocks)]
    anyspace = pl.BlockSpec(memory_space=pl.ANY)
    smem = pl.BlockSpec(memory_space=pltpu.SMEM)
    V = pltpu.VMEM
    ZT = d.Z * T
    grads = jax.ShapeDtypeStruct((d.CAP, BLK, BLK), BF)
    act = jax.ShapeDtypeStruct((T, F), BF)
    shapes = [act, act, grads, grads, grads]
    results = pl.pallas_call(
        functools.partial(main_kernel, d),
        out_shape=shapes,
        in_specs=[smem] * 3 + [anyspace] * 5,
        out_specs=[anyspace] * 5,
        scratch_shapes=[
            pltpu.SMEM((3 * d.SL,), jnp.int32),
            *[V((d.CAP + 1, BLK, BLK), BF)] * 3,
            V((F, 2 * HU), BF),
            V((HU, F), BF),
            V((2, 2 * R, F), BF),
            V((2, R, F), BF),
            V((d.HALF, N), BF),
            V((d.HALF, N), BF),
            V((d.HALF, N), F32),
            V((7, T, N), BF),
            V((7, T, N), BF),
            V((T, N), F32),
            V((2 * R, N), BF),
            V((R, 2 * F), F32),
            V((2, 3, ZT, F), BF),
            V((2, 3, ZT, F), BF),
            V((ZT, 2 * F), F32),
            V((2, ZT, F), BF),
            V((2, d.Z - 1, T, F), BF),
            V((T, 2 * F), BF),
            V((F, 2 * R), BF),
            V((HU, 2 * R), BF),
            V((F, 2 * HU), F32),
            V((HU, F), F32),
            *[V((d.SL + 1, BLK, BLK), BF)] * 3,
            *[V((d.CAP, BLK, BLK), BF)] * 3,
            pltpu.SemaphoreType.DMA((5,)),
            pltpu.SemaphoreType.DMA((d.NSEM,)),
            pltpu.SemaphoreType.DMA((d.NSEM,)),
        ],
        compiler_params=pltpu.CompilerParams(
            collective_id=0, has_side_effects=True, vmem_limit_bytes=60 * 1024 * 1024
        ),
        name="ffn_main",
    )(*listings, tokens, cotangent, *blocks)
    o, ig, gg, ug, dgr = pl.pallas_call(
        pass_kernel,
        out_shape=shapes,
        in_specs=[anyspace] * 5,
        out_specs=[anyspace] * 5,
        scratch_shapes=[V(s.shape, BF) for s in shapes]
        + [pltpu.SemaphoreType.DMA((5,)), pltpu.SemaphoreType.DMA((5,))],
        compiler_params=pltpu.CompilerParams(vmem_limit_bytes=60 * 1024 * 1024),
        name="ffn_pass",
    )(*results)
    shape = gate_blocks.shape
    return (o, ig, gg.reshape(shape), ug.reshape(shape), dgr.reshape(shape))


def build(mesh, units):
    def body(tokens, cotangent, *rest):
        d = Dims(mesh.shape, tokens.shape[0], tokens.shape[1], rest[0].shape[2], units)
        return on_device(d, tokens, cotangent, *rest)

    act = P(("dp", "col"), "row")
    blocks = P("row", "col", None, None, None)
    index = P("row", "col", None, None)
    return jax.shard_map(
        body,
        mesh=mesh,
        in_specs=(act, act, blocks, index, blocks, index, blocks, index),
        out_specs=(act, act, blocks, blocks, blocks),
        check_vma=False,
    )


def solution(mesh):
    return build(mesh, 7)
```

```python
import functools
import math

import jax
import jax.numpy as jnp
from jax import lax
from jax.experimental import pallas as pl
from jax.experimental.pallas import tpu as pltpu
from jax.sharding import PartitionSpec as P

BLK = 128
XS = 4
MESH = pl.DeviceIdType.MESH
BF = jnp.bfloat16
F32 = jnp.float32


def split_tiles(tiles, parts, whole=False):
    cuts = [(tiles * i) // parts for i in range(parts + 1)]
    if whole:
        cuts = sorted({t * (tiles // 3) + c for t in range(3) for c in (0, (tiles // 3 + 1) // 2)} | {tiles})
        parts = len(cuts) - 1
    return [(cuts[i] * BLK, cuts[i + 1] * BLK, -1 if i % 2 == 0 else 1) for i in range(parts)]


class Dims:
    def __init__(self, mesh_shape, tok_rows, feat, cap, units):
        self.T = tok_rows
        self.F = feat
        self.CAP = cap
        self.DB = feat // BLK
        self.FB = units
        self.HU = units * BLK
        self.N = 3 * self.HU
        self.X = XS
        self.Z = mesh_shape["col"] // XS
        self.Y = mesh_shape["row"] // 2
        assert self.Y == 8 and self.X == 4
        self.NCOL = mesh_shape["col"]
        self.NROW = mesh_shape["row"]
        self.R = self.NCOL * self.T
        self.HALF = self.Y * self.T
        self.SL = self.DB * self.FB
        self.RS = split_tiles(3 * self.FB, 6, True)
        h, c = self.HU, (self.FB + 1) // 2 * BLK
        self.AG = [[(0, c, -1), (c, h, 1)], [(h, 2 * h, -1), (2 * h, 3 * h, 1)]]
        self.NSEM = 256


def main_kernel(
    d, gi, ui, di, tok, cot, gb, ub, db,
    o_out, ig_out, g_out, u_out, d_out,
    inv, wb0, wb1, wb2, wgu, wd, xr, xp, psend, precv, s1, rsend, rrecv, tot, hall,
    po, xsend, xrecv, zs, zsend, zrecv, xt, ht, acc_gu, acc_d, dg, du, dd,
    lsem, ssem, rsem,
):
    g = lax.axis_index("dp")
    row = lax.axis_index("row")
    col = lax.axis_index("col")
    y, k = lax.div(row, 2), lax.rem(row, 2)
    x, z = lax.div(col, d.Z), lax.rem(col, d.Z)
    T, F, HU, N, R = d.T, d.F, d.HU, d.N, d.R
    GU = 2 * HU
    ZT = d.Z * T
    wblk = (wb0, wb1, wb2)

    def ym(v):
        return lax.rem(y + v + 2 * d.Y, d.Y)

    def xm(v):
        return lax.rem(x + v + 2 * d.X, d.X)

    def zm(v):
        return lax.rem(z + v + 2 * d.Z, d.Z)

    def rows(start, size):
        return pl.ds(pl.multiple_of(start, size), size)

    def at_y(v):
        return {"row": ym(v) * 2 + k}

    def at_x(v):
        return {"col": xm(v) * d.Z + z}

    def at_z(v):
        return {"col": x * d.Z + zm(v)}

    def at_other_z(v):
        return {"dp": 1 - g, "col": x * d.Z + zm(v)}

    partner = {"row": y * 2 + 1 - k}

    sent = []
    ids = {}

    def number(name):
        if name not in ids:
            ids[name] = len(ids)
            assert len(ids) <= d.NSEM
        return ids[name]

    def send(name, src, dst, dev):
        i = number(name)
        c = pltpu.make_async_remote_copy(
            src_ref=src, dst_ref=dst, send_sem=ssem.at[i], recv_sem=rsem.at[i],
            device_id=dev, device_id_type=MESH,
        )
        c.start()
        sent.append(c)

    def recv(name, landing, dev):
        i = number(name)
        pltpu.make_async_remote_copy(
            src_ref=landing, dst_ref=landing, send_sem=ssem.at[i], recv_sem=rsem.at[i],
            device_id=dev, device_id_type=MESH,
        ).wait_recv()

    barrier = pltpu.get_barrier_semaphore()
    peers = [at_z(o) for o in range(1, d.Z)] + [at_other_z(o) for o in range(d.Z)]
    peers += [at_x(v) for v in range(1, d.X)] + [at_y(v) for v in (1, -1, 2, -2)] + [partner]
    for p in peers:
        pl.semaphore_signal(barrier, inc=1, device_id=p, device_id_type=MESH)

    own_rows = rows(col * T, T)
    loads = [
        pltpu.make_async_copy(tok, xr.at[0, own_rows], lsem.at[0]),
        pltpu.make_async_copy(cot, xr.at[1, own_rows], lsem.at[1]),
        pltpu.make_async_copy(gb, wb0.at[pl.ds(0, d.CAP)], lsem.at[2]),
        pltpu.make_async_copy(ub, wb1.at[pl.ds(0, d.CAP)], lsem.at[3]),
        pltpu.make_async_copy(db, wb2.at[pl.ds(0, d.CAP)], lsem.at[4]),
    ]
    for c in loads[:2]:
        c.start()

    pl.semaphore_wait(barrier, len(peers))

    def chunk(t, v, o):
        return xr.at[t, rows((xm(v) * d.Z + zm(-o)) * T, T)]

    def x_chunk(t, o, src):
        for v in (2, 1, -1):
            send(("xc", t, o, v), src, chunk(t, 0, o), at_x(v))

    def x_end(t, o):
        for v in (2, 1, -1):
            recv(("xc", t, o, v), chunk(t, -v, o), at_x(v))

    for t, src in ((0, tok), (1, cot)):
        for o in range(1, d.Z):
            send(("z0", t, o), src, xr.at[t, own_rows], at_z(o))
        x_chunk(t, 0, src)

    for c in loads[2:]:
        c.start()

    for t, (ref, per) in enumerate(((gi, d.FB), (ui, d.FB), (di, d.DB))):
        wblk[t][d.CAP] = jnp.zeros((BLK, BLK), BF)
        spots = [ref[0, s] * per + ref[1, s] for s in range(d.CAP)]

        def find(p, _, t=t, spots=spots):
            found = jnp.int32(d.CAP)
            for s in range(d.CAP):
                found = jnp.where(spots[s] == p, jnp.int32(s), found)
            inv[t * d.SL + p] = found
            return 0

        lax.fori_loop(0, d.SL, find, 0)

    def z_chunks(t):
        for o in range(1, d.Z):
            recv(("z0", t, o), chunk(t, 0, o), at_z(o))
            x_chunk(t, o, chunk(t, 0, o))

    def dense(t, per):
        loads[2 + t].wait()

        def put(p, _):
            i, j = lax.div(p, per), lax.rem(p, per)
            block = wblk[t][inv[t * d.SL + p]]
            if t < 2:
                wgu[rows(i * BLK, BLK), rows(j * BLK + t * HU, BLK)] = block
            else:
                wd[rows(i * BLK, BLK), rows(j * BLK, BLK)] = block
            return 0

        lax.fori_loop(0, d.SL, put, 0)

    z_chunks(0)
    z_chunks(1)

    other_rows = rows(R + col * T, T)
    for t, src in ((0, tok), (1, cot)):
        for o in range(d.Z):
            send(("z1", t, o), src, xr.at[t, other_rows], at_other_z(o))

    def z_other(t):
        for o in range(d.Z):
            recv(("z1", t, o), xr.at[t, rows(R + (x * d.Z + zm(-o)) * T, T)], at_z(o))

    def xblock(t, v):
        return xr.at[t, rows(R + xm(v) * ZT, ZT)]

    def b_send(t):
        for v in (2, 1, -1):
            send(("xb", t, v), xblock(t, 0), xblock(t, 0), at_x(v))

    def b_end(t):
        for v in (2, 1, -1):
            recv(("xb", t, v), xblock(t, -v), at_x(v))

    dense(0, d.FB)
    dense(1, d.FB)
    dense(2, d.DB)
    loads[0].wait()
    loads[1].wait()

    def nt(a, b):
        return lax.dot_general(a, b, (((1,), (1,)), ((), ())), preferred_element_type=F32)

    def nn(a, b):
        return jnp.dot(a, b, preferred_element_type=F32)

    H = d.HALF

    def halves(t):
        for o in range(d.Z):
            x_end(t, o)
        xp[t, 0:H] = xr[t, rows((1 - k) * H, H), :]
        xp[t, H : 2 * H] = xr[t, rows(k * H, H), :]

    def partial(q):
        a, b, _ = d.RS[q]
        part = nn(xp[0], wgu[:, a:b]) if b <= GU else nt(xp[1], wd[a - GU : b - GU, :])
        psend[:, a:b] = part[0:H].astype(BF)
        send(("p", q), psend.at[:, a:b], precv.at[:, a:b], partner)
        s1[:, a:b] = part[H : 2 * H]

    def rs_first(slot, q, m, far, hop):
        a, b, _ = d.RS[q]
        rsend[slot, :, a:b] = s1[rows(ym(m * far) * T, T), a:b].astype(BF)
        send(("r", slot, q), rsend.at[slot, :, a:b], rrecv.at[slot, :, a:b], at_y(m * hop))

    def rs_got(slot, q, m, hop):
        a, b, _ = d.RS[q]
        recv(("r", slot, q), rrecv.at[slot, :, a:b], at_y(m * hop))
        return rrecv[slot, :, a:b].astype(F32)

    def rs_start(q):
        a, b, m = d.RS[q]
        recv(("p", q), precv.at[:, a:b], partner)
        s1[:, a:b] += precv[:, a:b].astype(F32)
        rs_first(0, q, m, 4, 2)
        rs_first(1, q, m, 3, 1)
        rs_first(4, q, -m, 3, 1)
        rs_first(3, q, m, 1, 1)
        rs_first(6, q, -m, 1, 1)

    def rs_second(q):
        a, b, m = d.RS[q]
        full = s1[rows(ym(2 * m) * T, T), a:b] + rs_got(0, q, m, 2) + rs_got(1, q, m, 1)
        rsend[2, :, a:b] = full.astype(BF)
        send(("r", 2, q), rsend.at[2, :, a:b], rrecv.at[2, :, a:b], at_y(2 * m))
        full = s1[rows(ym(-2 * m) * T, T), a:b] + rs_got(4, q, -m, 1)
        rsend[5, :, a:b] = full.astype(BF)
        send(("r", 5, q), rsend.at[5, :, a:b], rrecv.at[5, :, a:b], at_y(-2 * m))

    def rs_end(q):
        a, b, m = d.RS[q]
        full = s1[rows(y * T, T), a:b] + rs_got(3, q, m, 1) + rs_got(6, q, -m, 1)
        tot[:, a:b] = full + rs_got(2, q, m, 2) + rs_got(5, q, -m, 2)

    early = [q for q, (_, b, _) in enumerate(d.RS) if b <= GU]
    late = [q for q, (_, b, _) in enumerate(d.RS) if b > GU]
    for t, part in ((0, early), (1, late)):
        halves(t)
        for q in part:
            partial(q)
        for q in part:
            rs_start(q)
    for q in early + late:
        rs_second(q)
    for t in (0, 1):
        z_other(t)
        b_send(t)
    xt[:, 0:R] = xr[0, 0:R, :].T

    def hrows(gs, kk, yy):
        return rows(gs * R + (kk * d.Y + yy) * T, T)

    def ag_ref(gs, v, c):
        return hall.at[hrows(gs, k, ym(v)), c[0] : c[1]]

    def ag_send(gs, c, m, src, dst):
        ref = ag_ref(gs, -m * src, c)
        send(("a", gs, c[0], m * dst), ref, ref, at_y(m * (dst - src)))

    def ag_recv(gs, c, m, dst):
        recv(("a", gs, c[0], m * dst), ag_ref(gs, -m * dst, c), at_y(m))

    def to_partner(gs, grp, v):
        ref = ag_ref(gs, v, (d.AG[grp][0][0], d.AG[grp][-1][1]))
        send(("ap", gs, grp, v), ref, ref, partner)

    def ag_start(gs, grp):
        for dst in (2, 1):
            for c in d.AG[grp]:
                ag_send(gs, c, c[2], 0, dst)
                ag_send(gs, c, -c[2], 0, dst)
        to_partner(gs, grp, 0)

    def ag_step(gs, grp):
        for c in d.AG[grp]:
            m = c[2]
            ag_recv(gs, c, m, 2)
            ag_send(gs, c, m, 2, 3)
            ag_send(gs, c, m, 2, 4)
            ag_recv(gs, c, -m, 2)
            ag_send(gs, c, -m, 2, 3)
        for v in (2, -2):
            to_partner(gs, grp, v)
        for c in d.AG[grp]:
            ag_recv(gs, c, 1, 1)
            ag_recv(gs, c, -1, 1)
        for v in (1, -1):
            to_partner(gs, grp, v)

    def ag_last(gs, grp):
        for c in d.AG[grp]:
            ag_recv(gs, c, 1, 3)
            ag_recv(gs, c, -1, 3)
        for v in (3, -3):
            to_partner(gs, grp, v)
        for c in d.AG[grp]:
            ag_recv(gs, c, c[2], 4)
        to_partner(gs, grp, 4)

    def ag_partner(gs, grp):
        a, b = d.AG[grp][0][0], d.AG[grp][-1][1]
        for v in range(-3, 5):
            recv(("ap", gs, grp, v), hall.at[hrows(gs, 1 - k, ym(v)), a:b], partner)

    def over_dp(grp):
        cols = slice(0, HU) if grp == 0 else slice(HU, N)
        i = number(("dp", grp))
        return pltpu.make_async_remote_copy(
            src_ref=hall.at[mine_rows, cols], dst_ref=hall.at[hrows(1, k, y), cols], send_sem=ssem.at[i],
            recv_sem=rsem.at[i], device_id={"dp": 1 - g}, device_id_type=MESH,
        )

    def dp_landed(grp):
        cols = slice(0, HU) if grp == 0 else slice(HU, N)
        recv(("dp", grp), hall.at[hrows(1, k, y), cols], {"dp": 1 - g})
        sent.append(over_dp(grp))

    mine_rows = rows((k * d.Y + y) * T, T)
    for q in early:
        rs_end(q)
    gate, up = tot[:, 0:HU], tot[:, HU:GU]
    sig = jax.nn.sigmoid(gate)
    hall[mine_rows, 0:HU] = (gate * sig * up).astype(BF)
    ag_start(0, 0)
    over_dp(0).start()
    for q in late:
        rs_end(q)
    gate, up, gh = tot[:, 0:HU], tot[:, HU:GU], tot[:, GU:N]
    sig = jax.nn.sigmoid(gate)
    hall[mine_rows, HU:GU] = (gh * up * sig * (1.0 + gate * (1.0 - sig))).astype(BF)
    hall[mine_rows, GU:N] = (gh * gate * sig).astype(BF)
    ag_start(0, 1)
    over_dp(1).start()
    ag_step(0, 0)
    ag_step(0, 1)
    dp_landed(0)
    ag_start(1, 0)
    ag_last(0, 0)

    def xrows(v):
        return rows(xm(v) * ZT, ZT)

    FAR = (2, 1, -1)

    def x_copy(t, i):
        return pltpu.make_async_remote_copy(
            src_ref=xsend.at[t, i], dst_ref=xrecv.at[t, i], send_sem=ssem.at[number(("ox", t, i))],
            recv_sem=rsem.at[number(("ox", t, i))], device_id=at_x(FAR[i]), device_id_type=MESH,
        )

    def x_first(t, half):
        for i, v in enumerate(FAR):

            @pl.when(lax.div(xm(v), d.X // 2) == half)
            def _(i=i, v=v):
                xsend[t, i] = po[xrows(v), t * F : (t + 1) * F].astype(BF)
                x_copy(t, i).start()

    def x_last(t):
        a, b = t * F, (t + 1) * F
        full = po[xrows(0), a:b]
        for i, v in enumerate(FAR):
            recv(("ox", t, i), xrecv.at[t, i], at_x(v))
            full = full + xrecv[t, i].astype(F32)
        zs[:, a:b] = full
        zsend[t] = full.astype(BF)
        for o in range(1, d.Z):
            send(("oz", t, o), zsend.at[t, rows(zm(o) * T, T)], zrecv.at[t, o - 1], at_z(o))

    scale = 1.0 / math.sqrt(2 * R)
    WN = 2 * BLK

    def w_gu(gs, n):
        tk = slice(gs * R, gs * R + R)
        full = nn(xt[:, tk], hall[tk, HU + n : HU + n + WN])
        if gs == 0:
            acc_gu[:, n : n + WN] = full
            return
        full = ((full + acc_gu[:, n : n + WN]) * scale).astype(BF)
        for i in range(d.DB):
            for j in range(2):
                at = n // BLK + j
                dst, jj = (dg, at) if at < d.FB else (du, at - d.FB)
                dst[i * d.FB + jj] = full[i * BLK : (i + 1) * BLK, j * BLK : (j + 1) * BLK]

    def w_d(gs, n):
        tk = slice(gs * R, gs * R + R)
        full = nn(ht[:, tk], xr[1, tk, n : n + WN])
        if gs == 0:
            acc_d[:, n : n + WN] = full
            return
        full = ((full + acc_d[:, n : n + WN]) * scale).astype(BF)
        for i in range(d.FB):
            for j in range(2):
                dd[i * d.DB + n // BLK + j] = full[i * BLK : (i + 1) * BLK, j * BLK : (j + 1) * BLK]

    def o_half(half):
        rh = rows(half * H, H)
        po[rh, 0:F] = nn(hall[rh, 0:HU], wd[...])
        x_first(0, half)

    def ig_half(half):
        rh = rows(half * H, H)
        po[rh, F : 2 * F] = nt(hall[rh, HU:N], wgu[...])
        x_first(1, half)

    o_half(k)
    ag_partner(0, 0)
    o_half(1 - k)
    dp_landed(1)
    ag_start(1, 1)
    ag_last(0, 1)
    ig_half(k)
    ag_partner(0, 1)
    ig_half(1 - k)
    for t in (0, 1):
        for i in range(len(FAR)):
            sent.append(x_copy(t, i))
    steps = list(range(0, GU, WN))
    ag_step(1, 0)
    for n in steps:
        w_gu(0, n)
    ht[:, 0:R] = hall[0:R, 0:HU].T
    for n in range(0, F, WN):
        w_d(0, n)
    x_last(0)
    ag_step(1, 1)
    ag_last(1, 0)
    x_last(1)
    b_end(0)
    b_end(1)
    xt[:, R : 2 * R] = xr[0, R : 2 * R, :].T
    ag_partner(1, 0)
    ht[:, R : 2 * R] = hall[R : 2 * R, 0:HU].T
    for n in range(0, F, WN):
        w_d(1, n)
    ag_last(1, 1)
    ag_partner(1, 1)
    for buf in (dg, du, dd):
        buf[d.SL] = jnp.zeros((BLK, BLK), BF)

    def pick(ref, per, src, dst):
        for s in range(d.CAP):
            at = ref[0, s] * per + ref[1, s]
            dst[s] = src[jnp.where(at < 0, jnp.int32(d.SL), at)]

    pick(di, d.DB, dd, d_out)
    for n in steps:
        w_gu(1, n)
    pick(gi, d.FB, dg, g_out)
    pick(ui, d.FB, du, u_out)

    for t, out in ((0, o_out), (1, ig_out)):
        full = zs[rows(z * T, T), t * F : (t + 1) * F]
        for o in range(1, d.Z):
            recv(("oz", t, o), zrecv.at[t, o - 1], at_z(o))
            full = full + zrecv[t, o - 1].astype(F32)
        out[...] = full.astype(BF)
    for c in sent:
        c.wait_send()


def pass_kernel(*refs):
    n = 5
    copies = [pltpu.make_async_copy(refs[i], refs[n + i], refs[2 * n].at[i]) for i in range(n)]
    for c in copies:
        c.start()
    for c in copies:
        c.wait()


def on_device(d, tokens, cotangent, gate_blocks, gate_index, up_blocks, up_index, down_blocks, down_index):
    T, F, HU, N, R = d.T, d.F, d.HU, d.N, d.R
    listings = [a[0, 0].T for a in (gate_index, up_index, down_index)]
    blocks = [a[0, 0] for a in (gate_blocks, up_blocks, down_blocks)]
    anyspace = pl.BlockSpec(memory_space=pl.ANY)
    smem = pl.BlockSpec(memory_space=pltpu.SMEM)
    V = pltpu.VMEM
    ZT = d.Z * T
    grads = jax.ShapeDtypeStruct((d.CAP, BLK, BLK), BF)
    act = jax.ShapeDtypeStruct((T, F), BF)
    shapes = [act, act, grads, grads, grads]
    results = pl.pallas_call(
        functools.partial(main_kernel, d),
        out_shape=[pltpu.VMEM(q.shape, q.dtype) for q in shapes],
        in_specs=[smem] * 3 + [anyspace] * 5,
        out_specs=[pl.BlockSpec(memory_space=pltpu.VMEM)] * 5,
        scratch_shapes=[
            pltpu.SMEM((3 * d.SL,), jnp.int32),
            *[V((d.CAP + 1, BLK, BLK), BF)] * 3,
            V((F, 2 * HU), BF),
            V((HU, F), BF),
            V((2, 2 * R, F), BF),
            V((2, R, F), BF),
            V((d.HALF, N), BF),
            V((d.HALF, N), BF),
            V((d.HALF, N), F32),
            V((7, T, N), BF),
            V((7, T, N), BF),
            V((T, N), F32),
            V((2 * R, N), BF),
            V((R, 2 * F), F32),
            V((2, 3, ZT, F), BF),
            V((2, 3, ZT, F), BF),
            V((ZT, 2 * F), F32),
            V((2, ZT, F), BF),
            V((2, d.Z - 1, T, F), BF),
            V((F, 2 * R), BF),
            V((HU, 2 * R), BF),
            V((F, 2 * HU), F32),
            V((HU, F), F32),
            *[V((d.SL + 1, BLK, BLK), BF)] * 3,
            pltpu.SemaphoreType.DMA((5,)),
            pltpu.SemaphoreType.DMA((d.NSEM,)),
            pltpu.SemaphoreType.DMA((d.NSEM,)),
        ],
        compiler_params=pltpu.CompilerParams(
            collective_id=0, has_side_effects=True, vmem_limit_bytes=52 * 1024 * 1024
        ),
        name="ffn_main",
    )(*listings, tokens, cotangent, *blocks)
    o, ig, gg, ug, dgr = pl.pallas_call(
        pass_kernel,
        out_shape=shapes,
        in_specs=[pl.BlockSpec(memory_space=pltpu.VMEM)] * 5,
        out_specs=[anyspace] * 5,
        scratch_shapes=[pltpu.SemaphoreType.DMA((5,))],
        compiler_params=pltpu.CompilerParams(vmem_limit_bytes=8 * 1024 * 1024),
        name="ffn_pass",
    )(*results)
    shape = gate_blocks.shape
    return (o, ig, gg.reshape(shape), ug.reshape(shape), dgr.reshape(shape))


def build(mesh, units):
    def body(tokens, cotangent, *rest):
        d = Dims(mesh.shape, tokens.shape[0], tokens.shape[1], rest[0].shape[2], units)
        return on_device(d, tokens, cotangent, *rest)

    act = P(("dp", "col"), "row")
    blocks = P("row", "col", None, None, None)
    index = P("row", "col", None, None)
    return jax.shard_map(
        body,
        mesh=mesh,
        in_specs=(act, act, blocks, index, blocks, index, blocks, index),
        out_specs=(act, act, blocks, blocks, blocks),
        check_vma=False,
    )


def solution(mesh):
    return build(mesh, 7)
```

```python
import functools
import math

import jax
import jax.numpy as jnp
from jax import lax
from jax.experimental import pallas as pl
from jax.experimental.pallas import tpu as pltpu
from jax.sharding import PartitionSpec as P

BLK = 128
XS = 4
MESH = pl.DeviceIdType.MESH
BF = jnp.bfloat16
F32 = jnp.float32


def split_tiles(tiles, parts, whole=False):
    cuts = [(tiles * i) // parts for i in range(parts + 1)]
    if whole:
        cuts = sorted({t * (tiles // 3) + c for t in range(3) for c in (0, (tiles // 3 + 1) // 2)} | {tiles})
        parts = len(cuts) - 1
    return [(cuts[i] * BLK, cuts[i + 1] * BLK, -1 if i % 2 == 0 else 1) for i in range(parts)]


class Dims:
    def __init__(self, mesh_shape, tok_rows, feat, cap, units):
        self.T = tok_rows
        self.F = feat
        self.CAP = cap
        self.DB = feat // BLK
        self.FB = units
        self.HU = units * BLK
        self.N = 3 * self.HU
        self.X = XS
        self.Z = mesh_shape["col"] // XS
        self.Y = mesh_shape["row"] // 2
        assert self.Y == 8 and self.X == 4
        self.NCOL = mesh_shape["col"]
        self.NROW = mesh_shape["row"]
        self.R = self.NCOL * self.T
        self.HALF = self.Y * self.T
        self.SL = self.DB * self.FB
        self.RS = split_tiles(3 * self.FB, 6, True)
        h, c = self.HU, (self.FB + 1) // 2 * BLK
        self.AG = [[(0, c, -1), (c, h, 1)], [(h, 2 * h, -1), (2 * h, 3 * h, 1)]]
        self.NSEM = 256


def main_kernel(
    d, gi, ui, di, tok, cot, gb, ub, db,
    o_out, ig_out, g_out, u_out, d_out,
    inv, wb0, wb1, wb2, wgu, wd, xr, xp, psend, precv, s1, rsend, rrecv, tot, hall,
    po, xsend, xrecv, zs, zsend, zrecv, xt, ht, acc_gu, acc_d, dg, du, dd,
    lsem, ssem, rsem,
):
    g = lax.axis_index("dp")
    row = lax.axis_index("row")
    col = lax.axis_index("col")
    y, k = lax.div(row, 2), lax.rem(row, 2)
    x, z = lax.div(col, d.Z), lax.rem(col, d.Z)
    T, F, HU, N, R = d.T, d.F, d.HU, d.N, d.R
    GU = 2 * HU
    ZT = d.Z * T
    wblk = (wb0, wb1, wb2)

    def ym(v):
        return lax.rem(y + v + 2 * d.Y, d.Y)

    def xm(v):
        return lax.rem(x + v + 2 * d.X, d.X)

    def zm(v):
        return lax.rem(z + v + 2 * d.Z, d.Z)

    def rows(start, size):
        return pl.ds(pl.multiple_of(start, size), size)

    def at_y(v):
        return {"row": ym(v) * 2 + k}

    def at_x(v):
        return {"col": xm(v) * d.Z + z}

    def at_z(v):
        return {"col": x * d.Z + zm(v)}

    def at_other_z(v):
        return {"dp": 1 - g, "col": x * d.Z + zm(v)}

    partner = {"row": y * 2 + 1 - k}

    sent = []
    ids = {}

    def number(name):
        if name not in ids:
            ids[name] = len(ids)
            assert len(ids) <= d.NSEM
        return ids[name]

    def send(name, src, dst, dev):
        i = number(name)
        c = pltpu.make_async_remote_copy(
            src_ref=src, dst_ref=dst, send_sem=ssem.at[i], recv_sem=rsem.at[i],
            device_id=dev, device_id_type=MESH,
        )
        c.start()
        sent.append(c)

    def recv(name, landing, dev):
        i = number(name)
        pltpu.make_async_remote_copy(
            src_ref=landing, dst_ref=landing, send_sem=ssem.at[i], recv_sem=rsem.at[i],
            device_id=dev, device_id_type=MESH,
        ).wait_recv()

    barrier = pltpu.get_barrier_semaphore()
    peers = [at_z(o) for o in range(1, d.Z)] + [at_other_z(o) for o in range(d.Z)]
    peers += [at_x(v) for v in range(1, d.X)] + [at_y(v) for v in (1, -1, 2, -2)] + [partner]
    for p in peers:
        pl.semaphore_signal(barrier, inc=1, device_id=p, device_id_type=MESH)

    own_rows = rows(col * T, T)
    loads = [
        pltpu.make_async_copy(tok, xr.at[0, own_rows], lsem.at[0]),
        pltpu.make_async_copy(cot, xr.at[1, own_rows], lsem.at[1]),
        pltpu.make_async_copy(gb, wb0.at[pl.ds(0, d.CAP)], lsem.at[2]),
        pltpu.make_async_copy(ub, wb1.at[pl.ds(0, d.CAP)], lsem.at[3]),
        pltpu.make_async_copy(db, wb2.at[pl.ds(0, d.CAP)], lsem.at[4]),
    ]
    for c in loads[:2]:
        c.start()

    pl.semaphore_wait(barrier, len(peers))

    def chunk(t, v, o):
        return xr.at[t, rows((xm(v) * d.Z + zm(-o)) * T, T)]

    def x_chunk(t, o, src):
        for v in (2, 1, -1):
            send(("xc", t, o, v), src, chunk(t, 0, o), at_x(v))

    def x_end(t, o):
        for v in (2, 1, -1):
            recv(("xc", t, o, v), chunk(t, -v, o), at_x(v))

    for t, src in ((0, tok), (1, cot)):
        for o in range(1, d.Z):
            send(("z0", t, o), src, xr.at[t, own_rows], at_z(o))
        x_chunk(t, 0, src)

    for c in loads[2:]:
        c.start()

    for t, (ref, per) in enumerate(((gi, d.FB), (ui, d.FB), (di, d.DB))):
        wblk[t][d.CAP] = jnp.zeros((BLK, BLK), BF)
        spots = [ref[0, s] * per + ref[1, s] for s in range(d.CAP)]

        def find(p, _, t=t, spots=spots):
            found = jnp.int32(d.CAP)
            for s in range(d.CAP):
                found = jnp.where(spots[s] == p, jnp.int32(s), found)
            inv[t * d.SL + p] = found
            return 0

        lax.fori_loop(0, d.SL, find, 0)

    def z_chunks(t):
        for o in range(1, d.Z):
            recv(("z0", t, o), chunk(t, 0, o), at_z(o))
            x_chunk(t, o, chunk(t, 0, o))

    def dense(t, per):
        loads[2 + t].wait()

        def put(p, _):
            i, j = lax.div(p, per), lax.rem(p, per)
            block = wblk[t][inv[t * d.SL + p]]
            if t < 2:
                wgu[rows(i * BLK, BLK), rows(j * BLK + t * HU, BLK)] = block
            else:
                wd[rows(i * BLK, BLK), rows(j * BLK, BLK)] = block
            return 0

        lax.fori_loop(0, d.SL, put, 0)

    z_chunks(0)
    z_chunks(1)

    other_rows = rows(R + col * T, T)
    for t, src in ((0, tok), (1, cot)):
        for o in range(d.Z):
            send(("z1", t, o), src, xr.at[t, other_rows], at_other_z(o))

    def z_other(t):
        for o in range(d.Z):
            recv(("z1", t, o), xr.at[t, rows(R + (x * d.Z + zm(-o)) * T, T)], at_z(o))

    def xblock(t, v):
        return xr.at[t, rows(R + xm(v) * ZT, ZT)]

    def b_send(t):
        for v in (2, 1, -1):
            send(("xb", t, v), xblock(t, 0), xblock(t, 0), at_x(v))

    def b_end(t):
        for v in (2, 1, -1):
            recv(("xb", t, v), xblock(t, -v), at_x(v))

    dense(0, d.FB)
    dense(1, d.FB)
    dense(2, d.DB)
    loads[0].wait()
    loads[1].wait()

    def nt(a, b):
        return lax.dot_general(a, b, (((1,), (1,)), ((), ())), preferred_element_type=F32)

    def nn(a, b):
        return jnp.dot(a, b, preferred_element_type=F32)

    H = d.HALF

    def halves(t):
        for o in range(d.Z):
            x_end(t, o)
        xp[t, 0:H] = xr[t, rows((1 - k) * H, H), :]
        xp[t, H : 2 * H] = xr[t, rows(k * H, H), :]

    def partial(q):
        a, b, _ = d.RS[q]
        part = nn(xp[0], wgu[:, a:b]) if b <= GU else nt(xp[1], wd[a - GU : b - GU, :])
        psend[:, a:b] = part[0:H].astype(BF)
        send(("p", q), psend.at[:, a:b], precv.at[:, a:b], partner)
        s1[:, a:b] = part[H : 2 * H]

    def rs_first(slot, q, m, far, hop):
        a, b, _ = d.RS[q]
        rsend[slot, :, a:b] = s1[rows(ym(m * far) * T, T), a:b].astype(BF)
        send(("r", slot, q), rsend.at[slot, :, a:b], rrecv.at[slot, :, a:b], at_y(m * hop))

    def rs_got(slot, q, m, hop):
        a, b, _ = d.RS[q]
        recv(("r", slot, q), rrecv.at[slot, :, a:b], at_y(m * hop))
        return rrecv[slot, :, a:b].astype(F32)

    def rs_start(q):
        a, b, m = d.RS[q]
        recv(("p", q), precv.at[:, a:b], partner)
        s1[:, a:b] += precv[:, a:b].astype(F32)
        rs_first(0, q, m, 4, 2)
        rs_first(1, q, m, 3, 1)
        rs_first(4, q, -m, 3, 1)
        rs_first(3, q, m, 1, 1)
        rs_first(6, q, -m, 1, 1)

    def rs_second(q):
        a, b, m = d.RS[q]
        full = s1[rows(ym(2 * m) * T, T), a:b] + rs_got(0, q, m, 2) + rs_got(1, q, m, 1)
        rsend[2, :, a:b] = full.astype(BF)
        send(("r", 2, q), rsend.at[2, :, a:b], rrecv.at[2, :, a:b], at_y(2 * m))
        full = s1[rows(ym(-2 * m) * T, T), a:b] + rs_got(4, q, -m, 1)
        rsend[5, :, a:b] = full.astype(BF)
        send(("r", 5, q), rsend.at[5, :, a:b], rrecv.at[5, :, a:b], at_y(-2 * m))

    def rs_end(q):
        a, b, m = d.RS[q]
        full = s1[rows(y * T, T), a:b] + rs_got(3, q, m, 1) + rs_got(6, q, -m, 1)
        tot[:, a:b] = full + rs_got(2, q, m, 2) + rs_got(5, q, -m, 2)

    early = [q for q, (_, b, _) in enumerate(d.RS) if b <= GU]
    late = [q for q, (_, b, _) in enumerate(d.RS) if b > GU]
    for t, part in ((0, early), (1, late)):
        halves(t)
        for q in part:
            partial(q)
        for q in part:
            rs_start(q)
    for q in early + late:
        rs_second(q)
    for t in (0, 1):
        z_other(t)
        b_send(t)
    xt[:, 0:R] = xr[0, 0:R, :].T

    def hrows(gs, kk, yy):
        return rows(gs * R + (kk * d.Y + yy) * T, T)

    def ag_ref(gs, v, c):
        return hall.at[hrows(gs, k, ym(v)), c[0] : c[1]]

    def ag_send(gs, c, m, src, dst):
        ref = ag_ref(gs, -m * src, c)
        send(("a", gs, c[0], m * dst), ref, ref, at_y(m * (dst - src)))

    def ag_recv(gs, c, m, dst):
        recv(("a", gs, c[0], m * dst), ag_ref(gs, -m * dst, c), at_y(m))

    def to_partner(gs, grp, v):
        ref = ag_ref(gs, v, (d.AG[grp][0][0], d.AG[grp][-1][1]))
        send(("ap", gs, grp, v), ref, ref, partner)

    def ag_start(gs, grp):
        for dst in (2, 1):
            for c in d.AG[grp]:
                ag_send(gs, c, c[2], 0, dst)
                ag_send(gs, c, -c[2], 0, dst)
        to_partner(gs, grp, 0)

    def ag_step(gs, grp):
        for c in d.AG[grp]:
            m = c[2]
            ag_recv(gs, c, m, 2)
            ag_send(gs, c, m, 2, 3)
            ag_send(gs, c, m, 2, 4)
            ag_recv(gs, c, -m, 2)
            ag_send(gs, c, -m, 2, 3)
        for v in (2, -2):
            to_partner(gs, grp, v)
        for c in d.AG[grp]:
            ag_recv(gs, c, 1, 1)
            ag_recv(gs, c, -1, 1)
        for v in (1, -1):
            to_partner(gs, grp, v)

    def ag_last(gs, grp):
        for c in d.AG[grp]:
            ag_recv(gs, c, 1, 3)
            ag_recv(gs, c, -1, 3)
        for v in (3, -3):
            to_partner(gs, grp, v)
        for c in d.AG[grp]:
            ag_recv(gs, c, c[2], 4)
        to_partner(gs, grp, 4)

    def ag_partner(gs, grp):
        a, b = d.AG[grp][0][0], d.AG[grp][-1][1]
        for v in range(-3, 5):
            recv(("ap", gs, grp, v), hall.at[hrows(gs, 1 - k, ym(v)), a:b], partner)

    def over_dp(grp):
        cols = slice(0, HU) if grp == 0 else slice(HU, N)
        i = number(("dp", grp))
        return pltpu.make_async_remote_copy(
            src_ref=hall.at[mine_rows, cols], dst_ref=hall.at[hrows(1, k, y), cols], send_sem=ssem.at[i],
            recv_sem=rsem.at[i], device_id={"dp": 1 - g}, device_id_type=MESH,
        )

    def dp_landed(grp):
        cols = slice(0, HU) if grp == 0 else slice(HU, N)
        recv(("dp", grp), hall.at[hrows(1, k, y), cols], {"dp": 1 - g})
        sent.append(over_dp(grp))

    mine_rows = rows((k * d.Y + y) * T, T)
    for q in early:
        rs_end(q)
    gate, up = tot[:, 0:HU], tot[:, HU:GU]
    sig = jax.nn.sigmoid(gate)
    hall[mine_rows, 0:HU] = (gate * sig * up).astype(BF)
    ag_start(0, 0)
    over_dp(0).start()
    for q in late:
        rs_end(q)
    gate, up, gh = tot[:, 0:HU], tot[:, HU:GU], tot[:, GU:N]
    sig = jax.nn.sigmoid(gate)
    hall[mine_rows, HU:GU] = (gh * up * sig * (1.0 + gate * (1.0 - sig))).astype(BF)
    hall[mine_rows, GU:N] = (gh * gate * sig).astype(BF)
    ag_start(0, 1)
    over_dp(1).start()
    ag_step(0, 0)
    ag_step(0, 1)
    dp_landed(0)
    ag_start(1, 0)
    ag_last(0, 0)

    def xrows(v):
        return rows(xm(v) * ZT, ZT)

    FAR = (2, 1, -1)

    def x_copy(t, i):
        return pltpu.make_async_remote_copy(
            src_ref=xsend.at[t, i], dst_ref=xrecv.at[t, i], send_sem=ssem.at[number(("ox", t, i))],
            recv_sem=rsem.at[number(("ox", t, i))], device_id=at_x(FAR[i]), device_id_type=MESH,
        )

    def x_first(t, half):
        for i, v in enumerate(FAR):

            @pl.when(lax.div(xm(v), d.X // 2) == half)
            def _(i=i, v=v):
                xsend[t, i] = po[xrows(v), t * F : (t + 1) * F].astype(BF)
                x_copy(t, i).start()

    def x_last(t):
        a, b = t * F, (t + 1) * F
        full = po[xrows(0), a:b]
        for i, v in enumerate(FAR):
            recv(("ox", t, i), xrecv.at[t, i], at_x(v))
            full = full + xrecv[t, i].astype(F32)
        zs[:, a:b] = full
        zsend[t] = full.astype(BF)
        for o in range(1, d.Z):
            send(("oz", t, o), zsend.at[t, rows(zm(o) * T, T)], zrecv.at[t, o - 1], at_z(o))

    scale = 1.0 / math.sqrt(2 * R)
    WN = 2 * BLK

    def w_gu(gs, n):
        tk = slice(gs * R, gs * R + R)
        full = nn(xt[:, tk], hall[tk, HU + n : HU + n + WN])
        if gs == 0:
            acc_gu[:, n : n + WN] = full
            return
        full = ((full + acc_gu[:, n : n + WN]) * scale).astype(BF)
        for i in range(d.DB):
            for j in range(2):
                at = n // BLK + j
                dst, jj = (dg, at) if at < d.FB else (du, at - d.FB)
                dst[i * d.FB + jj] = full[i * BLK : (i + 1) * BLK, j * BLK : (j + 1) * BLK]

    def w_d(gs, n):
        tk = slice(gs * R, gs * R + R)
        full = nn(ht[:, tk], xr[1, tk, n : n + WN])
        if gs == 0:
            acc_d[:, n : n + WN] = full
            return
        full = ((full + acc_d[:, n : n + WN]) * scale).astype(BF)
        for i in range(d.FB):
            for j in range(2):
                dd[i * d.DB + n // BLK + j] = full[i * BLK : (i + 1) * BLK, j * BLK : (j + 1) * BLK]

    def o_half(half):
        rh = rows(half * H, H)
        po[rh, 0:F] = nn(hall[rh, 0:HU], wd[...])
        x_first(0, half)

    def ig_half(half):
        rh = rows(half * H, H)
        po[rh, F : 2 * F] = nt(hall[rh, HU:N], wgu[...])
        x_first(1, half)

    o_half(k)
    ag_partner(0, 0)
    o_half(1 - k)
    dp_landed(1)
    ag_start(1, 1)
    ag_last(0, 1)
    ig_half(k)
    ag_partner(0, 1)
    ig_half(1 - k)
    for t in (0, 1):
        for i in range(len(FAR)):
            sent.append(x_copy(t, i))
    steps = list(range(0, GU, WN))
    ag_step(1, 0)
    ag_step(1, 1)
    for n in steps:
        w_gu(0, n)
    ht[:, 0:R] = hall[0:R, 0:HU].T
    for n in range(0, F, WN):
        w_d(0, n)
    x_last(0)
    x_last(1)
    ag_last(1, 0)
    b_end(0)
    b_end(1)
    xt[:, R : 2 * R] = xr[0, R : 2 * R, :].T
    ag_partner(1, 0)
    ht[:, R : 2 * R] = hall[R : 2 * R, 0:HU].T
    for n in range(0, F, WN):
        w_d(1, n)
    ag_last(1, 1)
    ag_partner(1, 1)
    for buf in (dg, du, dd):
        buf[d.SL] = jnp.zeros((BLK, BLK), BF)

    def pick(ref, per, src, dst):
        for s in range(d.CAP):
            at = ref[0, s] * per + ref[1, s]
            dst[s] = src[jnp.where(at < 0, jnp.int32(d.SL), at)]

    pick(di, d.DB, dd, d_out)
    for n in steps:
        w_gu(1, n)
    pick(gi, d.FB, dg, g_out)
    pick(ui, d.FB, du, u_out)

    for t, out in ((0, o_out), (1, ig_out)):
        full = zs[rows(z * T, T), t * F : (t + 1) * F]
        for o in range(1, d.Z):
            recv(("oz", t, o), zrecv.at[t, o - 1], at_z(o))
            full = full + zrecv[t, o - 1].astype(F32)
        out[...] = full.astype(BF)
    for c in sent:
        c.wait_send()


def pass_kernel(*refs):
    n = 5
    copies = [pltpu.make_async_copy(refs[i], refs[n + i], refs[2 * n].at[i]) for i in range(n)]
    for c in copies:
        c.start()
    for c in copies:
        c.wait()


def on_device(d, tokens, cotangent, gate_blocks, gate_index, up_blocks, up_index, down_blocks, down_index):
    T, F, HU, N, R = d.T, d.F, d.HU, d.N, d.R
    listings = [a[0, 0].T for a in (gate_index, up_index, down_index)]
    blocks = [a[0, 0] for a in (gate_blocks, up_blocks, down_blocks)]
    anyspace = pl.BlockSpec(memory_space=pl.ANY)
    smem = pl.BlockSpec(memory_space=pltpu.SMEM)
    V = pltpu.VMEM
    ZT = d.Z * T
    grads = jax.ShapeDtypeStruct((d.CAP, BLK, BLK), BF)
    act = jax.ShapeDtypeStruct((T, F), BF)
    shapes = [act, act, grads, grads, grads]
    results = pl.pallas_call(
        functools.partial(main_kernel, d),
        out_shape=[pltpu.VMEM(q.shape, q.dtype) for q in shapes],
        in_specs=[smem] * 3 + [anyspace] * 5,
        out_specs=[pl.BlockSpec(memory_space=pltpu.VMEM)] * 5,
        scratch_shapes=[
            pltpu.SMEM((3 * d.SL,), jnp.int32),
            *[V((d.CAP + 1, BLK, BLK), BF)] * 3,
            V((F, 2 * HU), BF),
            V((HU, F), BF),
            V((2, 2 * R, F), BF),
            V((2, R, F), BF),
            V((d.HALF, N), BF),
            V((d.HALF, N), BF),
            V((d.HALF, N), F32),
            V((7, T, N), BF),
            V((7, T, N), BF),
            V((T, N), F32),
            V((2 * R, N), BF),
            V((R, 2 * F), F32),
            V((2, 3, ZT, F), BF),
            V((2, 3, ZT, F), BF),
            V((ZT, 2 * F), F32),
            V((2, ZT, F), BF),
            V((2, d.Z - 1, T, F), BF),
            V((F, 2 * R), BF),
            V((HU, 2 * R), BF),
            V((F, 2 * HU), F32),
            V((HU, F), F32),
            *[V((d.SL + 1, BLK, BLK), BF)] * 3,
            pltpu.SemaphoreType.DMA((5,)),
            pltpu.SemaphoreType.DMA((d.NSEM,)),
            pltpu.SemaphoreType.DMA((d.NSEM,)),
        ],
        compiler_params=pltpu.CompilerParams(
            collective_id=0, has_side_effects=True, vmem_limit_bytes=52 * 1024 * 1024
        ),
        name="ffn_main",
    )(*listings, tokens, cotangent, *blocks)
    o, ig, gg, ug, dgr = pl.pallas_call(
        pass_kernel,
        out_shape=shapes,
        in_specs=[pl.BlockSpec(memory_space=pltpu.VMEM)] * 5,
        out_specs=[anyspace] * 5,
        scratch_shapes=[pltpu.SemaphoreType.DMA((5,))],
        compiler_params=pltpu.CompilerParams(vmem_limit_bytes=8 * 1024 * 1024),
        name="ffn_pass",
    )(*results)
    shape = gate_blocks.shape
    return (o, ig, gg.reshape(shape), ug.reshape(shape), dgr.reshape(shape))


def build(mesh, units):
    def body(tokens, cotangent, *rest):
        d = Dims(mesh.shape, tokens.shape[0], tokens.shape[1], rest[0].shape[2], units)
        return on_device(d, tokens, cotangent, *rest)

    act = P(("dp", "col"), "row")
    blocks = P("row", "col", None, None, None)
    index = P("row", "col", None, None)
    return jax.shard_map(
        body,
        mesh=mesh,
        in_specs=(act, act, blocks, index, blocks, index, blocks, index),
        out_specs=(act, act, blocks, blocks, blocks),
        check_vma=False,
    )


def solution(mesh):
    return build(mesh, 7)
```
